32 devices in a mesh: grp: 2 (over y), src: 4 (over z), rcv: 4 (over x, core).
Axes of the slice: x: 2, y: 2, z: 4, core: 2. Of those that a mesh axis runs over, the one named last changes fastest.
Arguments:
- traces: bfloat16 [8, 1024, 2048], P(None, ('grp', 'rcv', 'src')), parts along dimension 1, may hold values from -120 to 120
- alive: int32 [8, 1024], P(None, ('grp', 'rcv', 'src')), parts along dimension 1, may hold values 0 or 1
- picks: int32 [32, 32], P(('grp', 'rcv', 'src')), parts along dimension 0, may hold values from 0 to 31, each once within a row
Outputs:
- correlations: bfloat16 [65, 256, 512], P(None, ('grp', 'src'), 'rcv'), parts along dimension 1
The draws below stay inside these ranges and needn't reach their ends.
There are 2 independent parts, one for each index of `grp`. The reference program is written for one: setup_inputs(seed, part) draws one part's arguments, and reference() takes and returns one part's arrays. A program takes and returns all parts, laid end to end along the dimension named above; each array names one. Nothing has to cross between parts.
Inputs may be any that keep to these rules, and one draw needn't show every extreme that they name: `picks`: row b belongs to the channel block of 32 channels numbered b along rcv+src (rcv the slower); it orders that block's channels, and its first 8 entries name the block's virtual sources.
All inputs are finite; a program needn't handle non-finite values. No bound on the sum of `alive` on one device may be relied on, other than what follows from the above.
Results may differ from the reference program's by a relative error of at most 0.0056.
Values may be sent and summed in bfloat16 or wider, within the bound.
No kernel may reach another device: no remote copies, remote signals or barrier semaphores. Data moves between devices by JAX's collectives and lax.ppermute only.
A program may use at most 64 MiB of HBM per device.

```python
import math
import jax
import jax.numpy as jnp
from jax import lax

SEGS = 8
SAMPLES = 2048
BINS = 256
LOWBIN = 16
MAXLAG = 32
LAGS = 65
RCV_DEV = 128
CH_DEV = 32
PICK = 8
SOURCES = 128
CHANNELS = 512
N_SRC = 4
N_RCV = 4


def draw_traces(key, part):
    key_base, key_chan, key_env = jax.random.split(key, 3)
    shape = (SEGS, CHANNELS, SAMPLES)
    base = jnp.clip(jax.random.normal(key_base, shape, jnp.float32), -4.0, 4.0)
    chan_scale = jnp.exp(jax.random.uniform(key_chan, (1, CHANNELS, 1), jnp.float32, 0.0, math.log(10.0)))
    envelope = jnp.exp(jax.random.uniform(key_env, shape, jnp.float32, 0.0, math.log(10.0)))
    return (0.2 * base * chan_scale * envelope).astype(jnp.bfloat16)


def with_ends(entries, stream_key, low, high):
    place = [jax.random.randint(jax.random.fold_in(stream_key, axis), (), 0, length) for axis, length in enumerate(entries.shape)]
    longest = entries.shape.index(max(entries.shape))
    neighbour = place[:longest] + [(place[longest] + 1) % entries.shape[longest]] + place[longest + 1:]
    return entries.at[tuple(place)].set(low).at[tuple(neighbour)].set(high)


def setup_inputs(seed: int = 0, part: int = 0) -> dict:
    streams_of = jax.random.split(jax.random.key(seed), 4)
    part_keys = jax.random.split(jax.random.fold_in(streams_of[3], part), 4)
    traces = draw_traces(jax.random.fold_in(jax.random.fold_in(streams_of[3], part), 71), part)
    alive = with_ends((jax.random.randint(part_keys[1], (SEGS, CHANNELS), 0, 8) < 7).astype(jnp.int32), jax.random.fold_in(part_keys[1], 1), 0, 1)
    picks = jax.vmap(lambda own: jax.random.permutation(own, CH_DEV))(jax.random.split(part_keys[2], (N_RCV * N_SRC))).reshape((N_RCV * N_SRC, CH_DEV)).astype(jnp.int32)
    return {"traces": traces, "alive": alive, "picks": picks}


def dft_table():
    sample_ids = jnp.arange(SAMPLES, dtype=jnp.int32)
    bin_ids = LOWBIN + jnp.arange(BINS, dtype=jnp.int32)
    angles = jnp.mod(sample_ids[:, None] * bin_ids[None, :], SAMPLES).astype(jnp.float32) * (2.0 * math.pi / SAMPLES)
    hann_taper = 0.5 - 0.5 * jnp.cos(sample_ids.astype(jnp.float32) * (2.0 * math.pi / SAMPLES))
    joined = jnp.concatenate([hann_taper[:, None] * jnp.cos(angles), -hann_taper[:, None] * jnp.sin(angles)], axis=1)
    return joined.astype(jnp.bfloat16)

def lag_tables():
    shifts = jnp.arange(LAGS, dtype=jnp.int32) - MAXLAG
    bin_ids = LOWBIN + jnp.arange(BINS, dtype=jnp.int32)
    angles = jnp.mod(shifts[:, None] * bin_ids[None, :], SAMPLES).astype(jnp.float32) * (2.0 * math.pi / SAMPLES)
    lag_scale = 1.0 / math.sqrt(SEGS * BINS)
    return (lag_scale * jnp.cos(angles), -lag_scale * jnp.sin(angles))

def spectra(samples, live, transform):
    seg_count, row_count = (samples.shape[0], samples.shape[1])
    raw_spec = jnp.dot(samples.reshape(seg_count * row_count, SAMPLES), transform, preferred_element_type=jnp.float32)
    mean_square = lax.optimization_barrier(jnp.mean(jnp.square(samples.astype(jnp.float32)), axis=-1)).reshape(seg_count * row_count, 1)
    weight = live.reshape(seg_count * row_count, 1).astype(jnp.float32) / jnp.sqrt(SAMPLES * (mean_square + 1e-06))
    return (raw_spec * weight).reshape(seg_count, row_count, 2 * BINS).astype(jnp.bfloat16)

def correlate(sources, receivers, cosine_lag_table, sine_lag_table):
    seg_count, src_count = (sources.shape[0], sources.shape[1])
    receiver_count = receivers.shape[1]
    source_block_view = sources.reshape(seg_count, src_count, 2, BINS).transpose(3, 1, 0, 2).reshape(BINS, src_count, 2 * seg_count)
    receiver_view = receivers.reshape(seg_count, receiver_count, 2, BINS)
    real_part = receiver_view[:, :, 0, :]
    imag_part = receiver_view[:, :, 1, :]
    real_cols = jnp.stack([real_part, imag_part], axis=1)
    imag_cols = jnp.stack([-imag_part, real_part], axis=1)
    column_entries = jnp.concatenate([real_cols, imag_cols], axis=2).transpose(3, 0, 1, 2).reshape(BINS, 2 * seg_count, 2 * receiver_count)
    spectral_sum_total = jnp.einsum('cni,cip->cnp', source_block_view.astype(jnp.float32), column_entries.astype(jnp.float32))
    summed_result = jnp.einsum('iy,yhp->ihp', cosine_lag_table, spectral_sum_total[:, :, :receiver_count], precision=lax.Precision.HIGHEST)
    summed_result = summed_result + jnp.einsum('iy,yhp->ihp', sine_lag_table, spectral_sum_total[:, :, receiver_count:], precision=lax.Precision.HIGHEST)
    return summed_result

def reference(traces, alive, picks):
    transform = dft_table()
    cosine_lag_table, sine_lag_table = lag_tables()
    local_spec = spectra(traces, alive, transform)
    chosen = picks[:, :PICK].reshape(N_RCV, N_SRC, PICK)
    block_ids = (jnp.arange(N_RCV, dtype=jnp.int32)[:, None] * N_SRC + jnp.arange(N_SRC, dtype=jnp.int32)[None, :]) * CH_DEV
    source_channels = (block_ids[:, :, None] + chosen).transpose(1, 0, 2).reshape(SOURCES).astype(jnp.int32)
    sources = jnp.take(local_spec, source_channels, axis=1)
    panels = local_spec.reshape(SEGS, N_RCV, RCV_DEV, 2 * BINS).transpose(1, 0, 2, 3)
    results = lax.map(lambda panel: correlate(sources, panel, cosine_lag_table, sine_lag_table), panels)
    joined = results.transpose(1, 2, 0, 3).reshape(LAGS, SOURCES, CHANNELS)
    return joined.astype(jnp.bfloat16)
```

```python
import functools
import math

import ml_dtypes
import numpy as np

import jax
import jax.numpy as jnp
from jax import lax
from jax.experimental import pallas as pl
from jax.experimental.pallas import tpu as pltpu
from jax.sharding import PartitionSpec as P

BINS = 256
LOWBIN = 16
MAXLAG = 32
LAGS = 2 * MAXLAG + 1
HALF = MAXLAG // 2
SRC_DEV = 32
KPARTS = 4


def dft_table(samples):
    t = np.arange(samples, dtype=np.int64)
    k = LOWBIN + np.arange(BINS, dtype=np.int64)
    angle = ((t[:, None] * k[None, :]) % samples) * (2.0 * np.pi / samples)
    taper = (0.5 - 0.5 * np.cos(t * (2.0 * np.pi / samples)))[:, None]
    joined = np.concatenate([taper * np.cos(angle), -taper * np.sin(angle)], axis=1)
    return joined.astype(np.float32).astype(ml_dtypes.bfloat16)


def phase_table(samples, shifts):
    k = LOWBIN + np.arange(BINS, dtype=np.int64)
    angle = ((np.asarray(shifts)[:, None] * k[None, :]) % samples) * (2.0 * np.pi / samples)
    return np.stack([np.cos(angle), np.sin(angle)], axis=1).astype(np.float32)


def spectra_kernel(x_hbm, w_hbm, alive_ref, picks_ref, spec_ref, src_ref, x_buf, w_buf, full, x_sem, w_sem):
    segs, chans, samples = x_hbm.shape
    rows = segs * chans
    step = samples // KPARTS
    copies = []
    for i in range(KPARTS):
        part = pl.ds(i * step, step)
        cx = pltpu.make_async_copy(x_hbm.at[:, :, part], x_buf.at[i], x_sem.at[i])
        cw = pltpu.make_async_copy(w_hbm.at[part, :], w_buf.at[i], w_sem.at[i])
        cx.start()
        cw.start()
        copies.append((cx, cw))
    total = None
    square = None
    for i in range(KPARTS):
        copies[i][0].wait()
        copies[i][1].wait()
        x = x_buf[i].reshape(rows, step)
        term = jnp.dot(x, w_buf[i], preferred_element_type=jnp.float32)
        xf = x.astype(jnp.float32)
        sq = jnp.sum(xf * xf, axis=1, keepdims=True)
        total = term if total is None else total + term
        square = sq if square is None else square + sq
    mean_square = square * (1.0 / samples)
    weight = alive_ref[...] / jnp.sqrt(samples * (mean_square + 1e-06))
    rounded = (total * weight).astype(jnp.bfloat16)
    spec_ref[...] = rounded.reshape(segs, chans, 2 * BINS)
    full[...] = rounded.astype(jnp.float32).reshape(segs, chans, 2 * BINS)
    for j in range(src_ref.shape[1]):
        src_ref[:, j : j + 1, :] = full[:, pl.ds(picks_ref[0, j], 1), :].astype(jnp.bfloat16)


def spectra(traces, alive, picks, pick_count):
    segs, chans, samples = traces.shape
    step = samples // KPARTS
    table = jnp.asarray(dft_table(samples))
    live = alive.astype(jnp.float32).reshape(segs * chans, 1)
    return pl.pallas_call(
        spectra_kernel,
        out_shape=(
            jax.ShapeDtypeStruct((segs, chans, 2 * BINS), jnp.bfloat16),
            jax.ShapeDtypeStruct((segs, pick_count, 2 * BINS), jnp.bfloat16),
        ),
        in_specs=[
            pl.BlockSpec(memory_space=pl.ANY),
            pl.BlockSpec(memory_space=pl.ANY),
            pl.BlockSpec(memory_space=pltpu.VMEM),
            pl.BlockSpec(memory_space=pltpu.SMEM),
        ],
        out_specs=(pl.BlockSpec(memory_space=pltpu.VMEM), pl.BlockSpec(memory_space=pltpu.VMEM)),
        scratch_shapes=[
            pltpu.VMEM((KPARTS, segs, chans, step), jnp.bfloat16),
            pltpu.VMEM((KPARTS, step, 2 * BINS), jnp.bfloat16),
            pltpu.VMEM((segs, chans, 2 * BINS), jnp.float32),
            pltpu.SemaphoreType.DMA((KPARTS,)),
            pltpu.SemaphoreType.DMA((KPARTS,)),
        ],
        name="spectra",
    )(traces, table, live, picks)


def correlate_kernel(src_layout, rcv_layout, n_in, *refs):
    inputs, tab_ref, rot_ref, out_ref = refs[:n_in], refs[n_in], refs[n_in + 1], refs[n_in + 2]
    src_buf, rcv_buf, src_all, rot_all, rows_buf, src_sem, rcv_sem = refs[n_in + 3 :]
    segs = src_buf.shape[1]
    n_src, n_rcv = src_all.shape[1], rcv_buf.shape[0] * rcv_buf.shape[2]

    def fetch(layout, pieces, buf, sem):
        for i, (piece, (slot, when)) in enumerate(zip(pieces, layout)):
            place = slot() if slot is not None else 0
            if when is None:
                pltpu.make_async_copy(piece, buf.at[place], sem.at[i]).start()
            else:

                @pl.when(when())
                def _():
                    pltpu.make_async_copy(piece, buf.at[place], sem.at[i]).start()

        for i, (piece, (slot, when)) in enumerate(zip(pieces, layout)):
            place = slot() if slot is not None else 0
            if when is None:
                pltpu.make_async_copy(piece, buf.at[place], sem.at[i]).wait()
            else:

                @pl.when(when())
                def _():
                    pltpu.make_async_copy(piece, buf.at[place], sem.at[i]).wait()

    fetch(src_layout, inputs[: len(src_layout)], src_buf, src_sem)
    for g in range(segs):
        src_all[g] = src_buf[:, g].reshape(n_src, 2 * BINS)
    fetch(rcv_layout, inputs[len(src_layout) :], rcv_buf, rcv_sem)

    for g in range(segs):
        both = rcv_buf[:, g].reshape(n_rcv, 2 * BINS).astype(jnp.float32)
        p, q = both[:, :BINS], both[:, BINS:]
        for h in range(2):
            c, s = rot_ref[h, 0:1, :], rot_ref[h, 1:2, :]
            here = pl.ds(h * n_rcv, n_rcv)
            at = g * 2 * BINS
            rot_all[here, pl.ds(at, BINS)] = (p * c + q * s).astype(jnp.bfloat16)
            rot_all[here, pl.ds(at + BINS, BINS)] = (q * c - p * s).astype(jnp.bfloat16)

    scale = 1.0 / math.sqrt(segs * BINS)
    group = rows_buf.shape[0] // (2 * n_src)

    def product(count):
        return lax.dot_general(
            rows_buf[:count], rot_all[...], (((1,), (1,)), ((), ())), preferred_element_type=jnp.float32
        )

    def put(lag, value):
        if lag < LAGS:
            out_ref[lag] = (value * scale).astype(jnp.bfloat16)

    def fill(e, even_at, odd_at):
        c = jnp.broadcast_to(tab_ref[e, 0:1, :], (n_src, BINS)).astype(jnp.bfloat16)
        s = jnp.broadcast_to(tab_ref[e, 1:2, :], (n_src, BINS)).astype(jnp.bfloat16)
        for g in range(segs):
            a, b = src_all[g, :, :BINS], src_all[g, :, BINS:]
            first, second = pl.ds(g * 2 * BINS, BINS), pl.ds(g * 2 * BINS + BINS, BINS)
            rows_buf[pl.ds(even_at, n_src), first] = a * c
            rows_buf[pl.ds(even_at, n_src), second] = b * c
            if odd_at is not None:
                rows_buf[pl.ds(odd_at, n_src), first] = b * s
                rows_buf[pl.ds(odd_at, n_src), second] = -(a * s)

    fill(0, 0, None)
    centre = product(n_src)
    put(HALF, centre[:, :n_rcv])
    put(3 * HALF + 1, centre[:, n_rcv:])
    for start in range(1, HALF + 1, group):
        for i in range(group):
            fill(start + i, 2 * i * n_src, (2 * i + 1) * n_src)
        done = product(2 * group * n_src)
        for i in range(group):
            e = start + i
            even = done[2 * i * n_src : (2 * i + 1) * n_src]
            odd = done[(2 * i + 1) * n_src : (2 * i + 2) * n_src]
            less, more = even - odd, even + odd
            put(HALF + e, less[:, :n_rcv])
            put(HALF - e, more[:, :n_rcv])
            put(3 * HALF + 1 + e, less[:, n_rcv:])
            put(3 * HALF + 1 - e, more[:, n_rcv:])


def correlate(src_parts, rcv_parts, samples):
    src_layout = [(slot, when) for _, slot, when in src_parts]
    rcv_layout = [(slot, when) for _, slot, when in rcv_parts]
    arrays = [a for a, _, _ in src_parts] + [a for a, _, _ in rcv_parts]
    segs, src_rows, width = src_parts[0][0].shape
    rcv_rows = rcv_parts[0][0].shape[1]
    src_slots = SRC_DEV // src_rows
    rcv_slots = 1 if len(rcv_parts) == 1 else lax.axis_size("src")
    n_rcv = rcv_rows * rcv_slots
    group = 4
    tab = jnp.asarray(phase_table(samples, np.arange(HALF + 1)))
    rot = jnp.asarray(phase_table(samples, np.array([-HALF, HALF + 1])))
    return pl.pallas_call(
        functools.partial(correlate_kernel, src_layout, rcv_layout, len(arrays)),
        out_shape=jax.ShapeDtypeStruct((LAGS, SRC_DEV, n_rcv), jnp.bfloat16),
        in_specs=[pl.BlockSpec(memory_space=pl.ANY)] * len(arrays) + [pl.BlockSpec(memory_space=pltpu.VMEM)] * 2,
        out_specs=pl.BlockSpec(memory_space=pltpu.VMEM),
        scratch_shapes=[
            pltpu.VMEM((src_slots, segs, src_rows, width), jnp.bfloat16),
            pltpu.VMEM((rcv_slots, segs, rcv_rows, width), jnp.bfloat16),
            pltpu.VMEM((segs, SRC_DEV, width), jnp.bfloat16),
            pltpu.VMEM((2 * n_rcv, segs * width), jnp.bfloat16),
            pltpu.VMEM((2 * group * SRC_DEV, segs * width), jnp.bfloat16),
            pltpu.SemaphoreType.DMA((len(src_parts),)),
            pltpu.SemaphoreType.DMA((len(rcv_parts),)),
        ],
        compiler_params=pltpu.CompilerParams(vmem_limit_bytes=48 << 20),
        name="correlate",
    )(*arrays, tab, rot)


def gather_sources(x):
    n = lax.axis_size("rcv")
    if n != 4:
        return [(lax.all_gather(x, "rcv", axis=1, tiled=True), None, None)]
    parts = [(x, lambda: lax.axis_index("rcv"), None)]
    for k in range(1, n):
        moved = lax.ppermute(x, "rcv", [(i, i ^ k) for i in range(n)])
        parts.append((moved, lambda k=k: lax.axis_index("rcv") ^ k, None))
    return parts


def gather_receivers(x):
    n = lax.axis_size("src")
    if n != 4:
        return [(lax.all_gather(x, "src", axis=1, tiled=True), None, None)]

    def at(k):
        return lambda: lax.axis_index("src") ^ k

    def inner():
        return (lax.axis_index("src") == 1) | (lax.axis_index("src") == 2)

    def outer():
        return (lax.axis_index("src") == 0) | (lax.axis_index("src") == 3)

    far = lax.ppermute(x, "src", [(i, i ^ 2) for i in range(n)])
    near = lax.ppermute(x, "src", [(i, i ^ 1) for i in range(n)])
    relay = lax.ppermute(far, "src", [(1, 0), (2, 3)])
    middle = lax.ppermute(x, "src", [(1, 2), (2, 1)])
    return [(x, at(0), None), (near, at(1), None), (far, at(2), None), (middle, at(3), inner), (relay, at(3), outer)]


def shards(traces, alive, picks):
    spec, chosen = spectra(traces, alive, picks, SRC_DEV // lax.axis_size("rcv"))
    return correlate(gather_sources(chosen), gather_receivers(spec), traces.shape[2])


def solution(mesh):
    return jax.shard_map(
        shards,
        mesh=mesh,
        in_specs=(
            P(None, ("grp", "rcv", "src"), None),
            P(None, ("grp", "rcv", "src")),
            P(("grp", "rcv", "src"), None),
        ),
        out_specs=P(None, ("grp", "src"), "rcv"),
        check_vma=False,
    )
```

```python
import functools
import math

import ml_dtypes
import numpy as np

import jax
import jax.numpy as jnp
from jax import lax
from jax.experimental import pallas as pl
from jax.experimental.pallas import tpu as pltpu
from jax.sharding import PartitionSpec as P


BINS = 256
LOWBIN = 16
MAXLAG = 32
LAGS = 2 * MAXLAG + 1
HALF = MAXLAG // 2
SRC_DEV = 32
KPARTS = 4


def dft_table(samples):
    t = np.arange(samples, dtype=np.int64)
    k = LOWBIN + np.arange(BINS, dtype=np.int64)
    angle = ((t[:, None] * k[None, :]) % samples) * (2.0 * np.pi / samples)
    taper = (0.5 - 0.5 * np.cos(t * (2.0 * np.pi / samples)))[:, None]
    joined = np.concatenate([taper * np.cos(angle), -taper * np.sin(angle)], axis=1)
    return joined.astype(np.float32).astype(ml_dtypes.bfloat16)


def phase_table(samples, shifts):
    k = LOWBIN + np.arange(BINS, dtype=np.int64)
    angle = ((np.asarray(shifts)[:, None] * k[None, :]) % samples) * (2.0 * np.pi / samples)
    return np.stack([np.cos(angle), np.sin(angle)], axis=1).astype(np.float32)


def spectra_kernel(x_hbm, w_hbm, alive_ref, picks_ref, spec_ref, *refs):
    half_refs, (src_ref, x_buf, w_buf, full, x_sem, w_sem) = refs[:2], refs[2:]
    segs, chans, samples = x_hbm.shape
    rows = segs * chans
    step = samples // KPARTS
    copies = []
    for i in range(KPARTS):
        part = pl.ds(i * step, step)
        cx = pltpu.make_async_copy(x_hbm.at[:, :, part], x_buf.at[i], x_sem.at[i])
        cw = pltpu.make_async_copy(w_hbm.at[part, :], w_buf.at[i], w_sem.at[i])
        cx.start()
        cw.start()
        copies.append((cx, cw))
    diagonal = lax.broadcasted_iota(jnp.int32, (chans, chans), 0) == lax.broadcasted_iota(jnp.int32, (chans, chans), 1)
    live = []
    for g in range(segs):
        row = jnp.broadcast_to(alive_ref[g : g + 1, :].astype(jnp.float32), (chans, chans))
        live.append(jnp.sum(jnp.where(diagonal, row, 0.0), axis=1, keepdims=True))
    live = jnp.concatenate(live, axis=0)
    total = None
    square = None
    for i in range(KPARTS):
        copies[i][0].wait()
        copies[i][1].wait()
        x = x_buf[i].reshape(rows, step)
        term = jnp.dot(x, w_buf[i], preferred_element_type=jnp.float32)
        xf = x.astype(jnp.float32)
        sq = jnp.sum(xf * xf, axis=1, keepdims=True)
        total = term if total is None else total + term
        square = sq if square is None else square + sq
    mean_square = square * (1.0 / samples)
    weight = live / jnp.sqrt(samples * (mean_square + 1e-06))
    rounded = (total * weight).astype(jnp.bfloat16).reshape(segs, chans, 2 * BINS)
    spec_ref[...] = rounded
    half_refs[0][...] = rounded[: segs // 2]
    half_refs[1][...] = rounded[segs // 2 :]
    full[...] = rounded.astype(jnp.float32)
    for j in range(src_ref.shape[1]):
        src_ref[:, j : j + 1, :] = full[:, pl.ds(picks_ref[0, j], 1), :].astype(jnp.bfloat16)


def spectra(traces, alive, picks, pick_count):
    segs, chans, samples = traces.shape
    step = samples // KPARTS
    table = jnp.asarray(dft_table(samples))
    half = jax.ShapeDtypeStruct((segs // 2, chans, 2 * BINS), jnp.bfloat16)
    return pl.pallas_call(
        spectra_kernel,
        out_shape=(
            jax.ShapeDtypeStruct((segs, chans, 2 * BINS), jnp.bfloat16),
            half,
            half,
            jax.ShapeDtypeStruct((segs, pick_count, 2 * BINS), jnp.bfloat16),
        ),
        in_specs=[
            pl.BlockSpec(memory_space=pl.ANY),
            pl.BlockSpec(memory_space=pl.ANY),
            pl.BlockSpec(memory_space=pltpu.VMEM),
            pl.BlockSpec(memory_space=pltpu.SMEM),
        ],
        out_specs=(pl.BlockSpec(memory_space=pltpu.VMEM),) * 4,
        scratch_shapes=[
            pltpu.VMEM((KPARTS, segs, chans, step), jnp.bfloat16),
            pltpu.VMEM((KPARTS, step, 2 * BINS), jnp.bfloat16),
            pltpu.VMEM((segs, chans, 2 * BINS), jnp.float32),
            pltpu.SemaphoreType.DMA((KPARTS,)),
            pltpu.SemaphoreType.DMA((KPARTS,)),
        ],
        name="spectra",
    )(traces, table, alive, picks)


def correlate_kernel(src_layout, rcv_layout, n_in, *refs):
    inputs, tab_ref, rot_ref, out_ref = refs[:n_in], refs[n_in], refs[n_in + 1], refs[n_in + 2]
    src_buf, rcv_buf, src_all, rot_all, rows_buf, src_sem, rcv_sem = refs[n_in + 3 :]
    segs = src_buf.shape[1]
    n_src, n_rcv = src_all.shape[1], rcv_buf.shape[0] * rcv_buf.shape[2]

    def fetch(layout, pieces, buf, sem, wait):
        for i, (piece, (slot, when, seg)) in enumerate(zip(pieces, layout)):
            place = slot() if slot is not None else 0
            copy = pltpu.make_async_copy(piece, buf.at[place, pl.ds(seg, piece.shape[0])], sem.at[i])
            step = copy.wait if wait else copy.start
            if when is None:
                step()
            else:
                pl.when(when())(step)

    src_pieces, rcv_pieces = inputs[: len(src_layout)], inputs[len(src_layout) :]
    fetch(src_layout, src_pieces, src_buf, src_sem, False)
    fetch(rcv_layout, rcv_pieces, rcv_buf, rcv_sem, False)
    fetch(src_layout, src_pieces, src_buf, src_sem, True)
    for g in range(segs):
        src_all[g] = src_buf[:, g].reshape(n_src, 2 * BINS)
    fetch(rcv_layout, rcv_pieces, rcv_buf, rcv_sem, True)

    for g in range(segs):
        both = rcv_buf[:, g].reshape(n_rcv, 2 * BINS).astype(jnp.float32)
        p, q = both[:, :BINS], both[:, BINS:]
        for h in range(2):
            c, s = rot_ref[h, 0:1, :], rot_ref[h, 1:2, :]
            here = pl.ds(h * n_rcv, n_rcv)
            at = g * 2 * BINS
            rot_all[here, pl.ds(at, BINS)] = (p * c + q * s).astype(jnp.bfloat16)
            rot_all[here, pl.ds(at + BINS, BINS)] = (q * c - p * s).astype(jnp.bfloat16)

    scale = 1.0 / math.sqrt(segs * BINS)
    group = rows_buf.shape[0] // (2 * n_src)

    def product(count):
        return lax.dot_general(
            rows_buf[:count], rot_all[...], (((1,), (1,)), ((), ())), preferred_element_type=jnp.float32
        )

    def put(lag, value):
        if lag < LAGS:
            out_ref[lag] = (value * scale).astype(jnp.bfloat16)

    def fill(e, even_at, odd_at):
        c = jnp.broadcast_to(tab_ref[e, 0:1, :], (n_src, BINS)).astype(jnp.bfloat16)
        s = jnp.broadcast_to(tab_ref[e, 1:2, :], (n_src, BINS)).astype(jnp.bfloat16)
        for g in range(segs):
            a, b = src_all[g, :, :BINS], src_all[g, :, BINS:]
            first, second = pl.ds(g * 2 * BINS, BINS), pl.ds(g * 2 * BINS + BINS, BINS)
            rows_buf[pl.ds(even_at, n_src), first] = a * c
            rows_buf[pl.ds(even_at, n_src), second] = b * c
            if odd_at is not None:
                rows_buf[pl.ds(odd_at, n_src), first] = b * s
                rows_buf[pl.ds(odd_at, n_src), second] = -(a * s)

    fill(0, 0, None)
    centre = product(n_src)
    put(HALF, centre[:, :n_rcv])
    put(3 * HALF + 1, centre[:, n_rcv:])
    for start in range(1, HALF + 1, group):
        for i in range(group):
            fill(start + i, 2 * i * n_src, (2 * i + 1) * n_src)
        done = product(2 * group * n_src)
        for i in range(group):
            e = start + i
            even = done[2 * i * n_src : (2 * i + 1) * n_src]
            odd = done[(2 * i + 1) * n_src : (2 * i + 2) * n_src]
            less, more = even - odd, even + odd
            put(HALF + e, less[:, :n_rcv])
            put(HALF - e, more[:, :n_rcv])
            put(3 * HALF + 1 + e, less[:, n_rcv:])
            put(3 * HALF + 1 - e, more[:, n_rcv:])


def correlate(src_parts, rcv_parts, samples):
    src_layout = [part[1:] for part in src_parts]
    rcv_layout = [part[1:] for part in rcv_parts]
    arrays = [part[0] for part in src_parts + rcv_parts]
    spaces = [pltpu.HBM if part[4] else pl.ANY for part in src_parts + rcv_parts]
    src_layout = [part[1:4] for part in src_parts]
    rcv_layout = [part[1:4] for part in rcv_parts]
    segs, src_rows, width = src_parts[0][0].shape
    rcv_rows = rcv_parts[0][0].shape[1]
    src_slots = SRC_DEV // src_rows
    rcv_slots = 1 if len(rcv_parts) == 1 else lax.axis_size("src")
    n_rcv = rcv_rows * rcv_slots
    group = 4
    tab = jnp.asarray(phase_table(samples, np.arange(HALF + 1)))
    rot = jnp.asarray(phase_table(samples, np.array([-HALF, HALF + 1])))
    return pl.pallas_call(
        functools.partial(correlate_kernel, src_layout, rcv_layout, len(arrays)),
        out_shape=jax.ShapeDtypeStruct((LAGS, SRC_DEV, n_rcv), jnp.bfloat16),
        in_specs=[pl.BlockSpec(memory_space=space) for space in spaces] + [pl.BlockSpec(memory_space=pltpu.VMEM)] * 2,
        out_specs=pl.BlockSpec(memory_space=pltpu.VMEM),
        scratch_shapes=[
            pltpu.VMEM((src_slots, segs, src_rows, width), jnp.bfloat16),
            pltpu.VMEM((rcv_slots, segs, rcv_rows, width), jnp.bfloat16),
            pltpu.VMEM((segs, SRC_DEV, width), jnp.bfloat16),
            pltpu.VMEM((2 * n_rcv, segs * width), jnp.bfloat16),
            pltpu.VMEM((2 * group * SRC_DEV, segs * width), jnp.bfloat16),
            pltpu.SemaphoreType.DMA((len(src_parts),)),
            pltpu.SemaphoreType.DMA((len(rcv_parts),)),
        ],
        compiler_params=pltpu.CompilerParams(vmem_limit_bytes=48 << 20),
        name="correlate",
    )(*arrays, tab, rot)


def gather_sources(x):
    n = lax.axis_size("rcv")
    if n != 4:
        return [(lax.all_gather(x, "rcv", axis=1, tiled=True), None, None, 0, False)]
    parts = [(x, lambda: lax.axis_index("rcv"), None, 0, True)]
    for k in range(n - 1, 0, -1):
        moved = lax.ppermute(x, "rcv", [(i, i ^ k) for i in range(n)])
        parts.append((moved, lambda k=k: lax.axis_index("rcv") ^ k, None, 0, False))
    return parts


def gather_receivers(x, halves):
    n = lax.axis_size("src")
    if n != 4:
        return [(lax.all_gather(x, "src", axis=1, tiled=True), None, None, 0, False)]

    def at(k):
        return lambda: lax.axis_index("src") ^ k

    def inner():
        return (lax.axis_index("src") == 1) | (lax.axis_index("src") == 2)

    def outer():
        return (lax.axis_index("src") == 0) | (lax.axis_index("src") == 3)

    outward, inward = [(1, 0), (2, 3)], [(0, 1), (3, 2)]
    parts = [(x, at(0), None, 0, True)]
    parts.append((lax.ppermute(x, "src", outward), at(1), outer, 0, False))
    far = [lax.ppermute(h, "src", [(i, i ^ 2) for i in range(n)]) for h in halves]
    parts.append((lax.ppermute(x, "src", inward), at(1), inner, 0, False))
    parts.append((lax.ppermute(x, "src", [(1, 2), (2, 1)]), at(3), inner, 0, False))
    for i, piece in enumerate(far):
        seg = i * piece.shape[0]
        parts.append((piece, at(2), None, seg, False))
        parts.append((lax.ppermute(piece, "src", outward), at(3), outer, seg, False))
    return parts


def shards(traces, alive, picks):
    spec, first, second, chosen = spectra(traces, alive, picks, SRC_DEV // lax.axis_size("rcv"))
    return correlate(gather_sources(chosen), gather_receivers(spec, (first, second)), traces.shape[2])


def solution(mesh):
    return jax.shard_map(
        shards,
        mesh=mesh,
        in_specs=(
            P(None, ("grp", "rcv", "src"), None),
            P(None, ("grp", "rcv", "src")),
            P(("grp", "rcv", "src"), None),
        ),
        out_specs=P(None, ("grp", "src"), "rcv"),
        check_vma=False,
    )
```

```python
import functools
import math

import ml_dtypes
import numpy as np

import jax
import jax.numpy as jnp
from jax import lax
from jax.experimental import pallas as pl
from jax.experimental.pallas import tpu as pltpu
from jax.sharding import PartitionSpec as P


BINS = 256
LOWBIN = 16
MAXLAG = 32
LAGS = 2 * MAXLAG + 1
BASE = 5
SPACING = 2 * BASE + 1
CENTRES = 7
SPLIT = 4
SRC_DEV = 32
KPARTS = 4


def dft_table(samples):
    t = np.arange(samples, dtype=np.int64)
    k = LOWBIN + np.arange(BINS, dtype=np.int64)
    angle = ((t[:, None] * k[None, :]) % samples) * (2.0 * np.pi / samples)
    taper = (0.5 - 0.5 * np.cos(t * (2.0 * np.pi / samples)))[:, None]
    joined = np.concatenate([taper * np.cos(angle), -taper * np.sin(angle)], axis=1)
    return joined.astype(np.float32).astype(ml_dtypes.bfloat16)


def phase_table(samples, shifts):
    k = LOWBIN + np.arange(BINS, dtype=np.int64)
    angle = ((np.asarray(shifts)[:, None] * k[None, :]) % samples) * (2.0 * np.pi / samples)
    return np.stack([np.cos(angle), np.sin(angle)], axis=1).astype(np.float32)


def spectra_kernel(start, last, x_hbm, w_hbm, alive_ref, *refs):
    count, chans, step = refs[-4].shape[1:4]
    samples = x_hbm.shape[2]
    rows = count * chans
    x_buf, w_buf, x_sem, w_sem = refs[-4:]
    copies = []
    for i in range(KPARTS):
        part = pl.ds(i * step, step)
        cx = pltpu.make_async_copy(x_hbm.at[pl.ds(start, count), :, part], x_buf.at[i], x_sem.at[i])
        cw = pltpu.make_async_copy(w_hbm.at[part, :], w_buf.at[i], w_sem.at[i])
        cx.start()
        cw.start()
        copies.append((cx, cw))
    diagonal = lax.broadcasted_iota(jnp.int32, (chans, chans), 0) == lax.broadcasted_iota(jnp.int32, (chans, chans), 1)
    live = []
    for g in range(start, start + count):
        row = jnp.broadcast_to(alive_ref[g : g + 1, :].astype(jnp.float32), (chans, chans))
        live.append(jnp.sum(jnp.where(diagonal, row, 0.0), axis=1, keepdims=True))
    live = jnp.concatenate(live, axis=0)
    total = None
    square = None
    for i in range(KPARTS):
        copies[i][0].wait()
        copies[i][1].wait()
        x = x_buf[i].reshape(rows, step)
        term = jnp.dot(x, w_buf[i], preferred_element_type=jnp.float32)
        xf = x.astype(jnp.float32)
        sq = jnp.sum(xf * xf, axis=1, keepdims=True)
        total = term if total is None else total + term
        square = sq if square is None else square + sq
    mean_square = square * (1.0 / samples)
    weight = live / jnp.sqrt(samples * (mean_square + 1e-06))
    rounded = (total * weight).astype(jnp.bfloat16).reshape(count, chans, 2 * BINS)
    if not last:
        refs[0][...] = rounded
        return
    early_ref, picks_ref, part_ref, spec_ref, src_ref, full = refs[:6]
    part_ref[...] = rounded
    early = early_ref[...]
    spec_ref[:start] = early
    spec_ref[start:] = rounded
    full[:start] = early.astype(jnp.float32)
    full[start:] = rounded.astype(jnp.float32)
    for j in range(src_ref.shape[1]):
        src_ref[:, j : j + 1, :] = full[:, pl.ds(picks_ref[0, j], 1), :].astype(jnp.bfloat16)


def spectra(traces, alive, picks, pick_count, split):
    segs, chans, samples = traces.shape
    step = samples // KPARTS
    table = jnp.asarray(dft_table(samples))
    vmem, anywhere = pl.BlockSpec(memory_space=pltpu.VMEM), pl.BlockSpec(memory_space=pl.ANY)

    def scratch(count):
        return [
            pltpu.VMEM((KPARTS, count, chans, step), jnp.bfloat16),
            pltpu.VMEM((KPARTS, step, 2 * BINS), jnp.bfloat16),
            pltpu.SemaphoreType.DMA((KPARTS,)),
            pltpu.SemaphoreType.DMA((KPARTS,)),
        ]

    def spec(count, rows=chans):
        return jax.ShapeDtypeStruct((count, rows, 2 * BINS), jnp.bfloat16)

    early = pl.pallas_call(
        functools.partial(spectra_kernel, 0, False),
        out_shape=spec(split),
        in_specs=[anywhere, anywhere, vmem],
        out_specs=vmem,
        scratch_shapes=scratch(split),
        name="spectra_early",
    )(traces, table, alive)
    part, whole, chosen = pl.pallas_call(
        functools.partial(spectra_kernel, split, True),
        out_shape=(spec(segs - split), spec(segs), spec(segs, pick_count)),
        in_specs=[anywhere, anywhere, vmem, vmem, pl.BlockSpec(memory_space=pltpu.SMEM)],
        out_specs=(vmem,) * 3,
        scratch_shapes=[pltpu.VMEM((segs, chans, 2 * BINS), jnp.float32)] + scratch(segs - split),
        name="spectra_late",
    )(traces, table, alive, early, picks)
    return early, part, whole, chosen


def lag_kernel(blocks, src_slots, n_in, n_rcv, first, *refs):
    inputs = refs[:n_in]
    rest = list(refs[n_in:])
    tab_ref = rest.pop(0)
    if first:
        out_ref, rows_ref = rest.pop(0), rest.pop(0)
    else:
        rows_in, prev_ref, out_ref = rest.pop(0), rest.pop(0), rest.pop(0)
    rot, sums = rest.pop(0), rest.pop(0)
    width = 2 * BINS
    segs = rot.shape[1] // width
    block_rows = rot.shape[0] // CENTRES
    n_src = out_ref.shape[1]
    scale = 1.0 / math.sqrt(segs * BINS)
    if not first:
        rows_ref, rows_sem = rest.pop(0), rest.pop(0)
        fetch = pltpu.make_async_copy(rows_in, rows_ref, rows_sem)
        fetch.start()

    if first:
        src_all = rest.pop(0)
        for i, slot in enumerate(src_slots):
            piece = inputs[i]
            rows = piece.shape[1]
            at = slot() * rows if slot is not None else 0
            src_all[:, pl.ds(at, rows), :] = piece[...].astype(jnp.float32)
        for g in range(segs):
            a, b = src_all[g, :, :BINS].astype(jnp.bfloat16), src_all[g, :, BINS:].astype(jnp.bfloat16)
            one, two = pl.ds(g * width, BINS), pl.ds(g * width + BINS, BINS)
            for e in range(BASE + 1):
                c = jnp.broadcast_to(tab_ref[e, 0:1, :], (n_src, BINS)).astype(jnp.bfloat16)
                even = pl.ds(e * n_src, n_src)
                rows_ref[even, one] = a * c
                rows_ref[even, two] = b * c
                if e > 0:
                    s = jnp.broadcast_to(tab_ref[e, 1:2, :], (n_src, BINS)).astype(jnp.bfloat16)
                    odd = pl.ds((BASE + e) * n_src, n_src)
                    rows_ref[odd, one] = b * s
                    rows_ref[odd, two] = -(a * s)

    lane_slot = lax.broadcasted_iota(jnp.int32, (n_src, n_rcv), 1) // block_rows
    waited = first
    for number, (pieces, slot) in enumerate(blocks):
        for g in range(segs):
            here = [p for p in pieces if p[1] <= g < p[1] + p[2]]
            both = None
            for index, seg, _, row, when in here:
                value = inputs[index][g - seg, row : row + block_rows, :].astype(jnp.float32)
                both = value if both is None else jnp.where(when(), value, both)
            p, q = both[:, :BINS], both[:, BINS:]
            one, two = pl.ds(g * width, BINS), pl.ds(g * width + BINS, BINS)

            def keep(centre, real, imag):
                at = pl.ds(centre * block_rows, block_rows)
                rot[at, one] = real.astype(jnp.bfloat16)
                rot[at, two] = imag.astype(jnp.bfloat16)

            keep(0, p, q)
            for i in range(CENTRES // 2):
                c, s = tab_ref[BASE + 1 + i, 0:1, :], tab_ref[BASE + 1 + i, 1:2, :]
                pc, ps, qc, qs = p * c, p * s, q * c, q * s
                keep(2 * i + 1, pc + qs, qc - ps)
                keep(2 * i + 2, pc - qs, qc + ps)
        if not waited:
            fetch.wait()
            waited = True
        sums[:, : CENTRES * block_rows] = lax.dot_general(
            rows_ref[...], rot[...], (((1,), (1,)), ((), ())), preferred_element_type=jnp.float32
        )
        place = slot()
        mine = lane_slot == place
        slots = n_rcv // block_rows

        def put(lag, value, group):
            if not 0 <= lag < LAGS:
                return
            moved = pltpu.roll(value, lax.rem(place - group + slots, slots) * block_rows, 1) if slots > 1 else value
            if number == 0 and first:
                old = 0.0
            else:
                old = (out_ref if number > 0 else prev_ref)[lag].astype(jnp.float32)
            out_ref[lag] = jnp.where(mine, moved * scale, old).astype(jnp.bfloat16)

        for centre in range(CENTRES):
            tile, group = divmod(centre, slots)
            lanes = pl.ds(tile * n_rcv, n_rcv)
            shift = ((centre + 1) // 2) * SPACING * (1 if centre % 2 else -1)
            middle = MAXLAG + shift
            for e in range(BASE + 1):
                if not (0 <= middle + e < LAGS or 0 <= middle - e < LAGS):
                    continue
                even = sums[pl.ds(e * n_src, n_src), lanes]
                if e == 0:
                    put(middle, even, group)
                    continue
                odd = sums[pl.ds((BASE + e) * n_src, n_src), lanes]
                put(middle + e, even - odd, group)
                put(middle - e, even + odd, group)


def lags(blocks, arrays, samples, n_rcv, block_rows, src_slots=None, rows=None, prev=None):
    first = rows is None
    segs, width = arrays[-1].shape[0] if first else rows.shape[1] // (2 * BINS), 2 * BINS
    tab = jnp.asarray(phase_table(samples, list(range(BASE + 1)) + [SPACING * i for i in range(1, CENTRES // 2 + 1)]))
    row_shape = ((2 * BASE + 1) * SRC_DEV, segs * width)
    vmem = pl.BlockSpec(memory_space=pltpu.VMEM)
    out = jax.ShapeDtypeStruct((LAGS, SRC_DEV, n_rcv), jnp.bfloat16)
    tiles = pl.cdiv(CENTRES * block_rows, n_rcv)
    scratch = [pltpu.VMEM((CENTRES * block_rows, segs * width), jnp.bfloat16), pltpu.VMEM((row_shape[0], tiles * n_rcv), jnp.float32)]
    if first:
        scratch.append(pltpu.VMEM((segs, SRC_DEV, width), jnp.float32))
    else:
        scratch += [pltpu.VMEM(row_shape, jnp.bfloat16), pltpu.SemaphoreType.DMA(())]
    extra = [] if first else [rows, prev]
    return pl.pallas_call(
        functools.partial(lag_kernel, blocks, src_slots, len(arrays), n_rcv, first),
        out_shape=(out, jax.ShapeDtypeStruct(row_shape, jnp.bfloat16)) if first else out,
        in_specs=[vmem] * (len(arrays) + 1) + ([] if first else [pl.BlockSpec(memory_space=pl.ANY), vmem]),
        out_specs=(vmem, vmem) if first else vmem,
        scratch_shapes=scratch,
        compiler_params=pltpu.CompilerParams(vmem_limit_bytes=40 << 20),
        name="lags_first" if first else "lags_more",
    )(*arrays, tab, *extra)


def gather_sources(x):
    n = lax.axis_size("rcv")
    if n != 4:
        return [lax.all_gather(x, "rcv", axis=1, tiled=True)], [None]
    moved = [lax.ppermute(x, "rcv", [(i, i ^ k) for i in range(n)]) for k in range(1, n)]
    return [x] + moved, [lambda k=k: lax.axis_index("rcv") ^ k for k in range(n)]


def work(traces, alive, picks):
    segs, chans, samples = traces.shape
    n = lax.axis_size("src")
    n_rcv = n * chans
    early, late, whole, chosen = spectra(traces, alive, picks, SRC_DEV // lax.axis_size("rcv"), SPLIT)
    sources, src_slots = gather_sources(chosen)
    k = len(sources)
    if n != 4:
        panel = lax.all_gather(whole, "src", axis=1, tiled=True)
        size = n_rcv // 4
        blocks = [([(k, 0, segs, i * size, None)], lambda i=i: i) for i in range(4)]
        return lags(blocks, sources + [panel], samples, n_rcv, size, src_slots)[0]

    def at(j):
        return lambda: lax.axis_index("src") ^ j

    def inner():
        return (lax.axis_index("src") == 1) | (lax.axis_index("src") == 2)

    far = [lax.ppermute(h, "src", [(i, i ^ 2) for i in range(n)]) for h in (early, late)]
    near = lax.ppermute(whole, "src", [(i, i ^ 1) for i in range(n)])
    middle = lax.ppermute(whole, "src", [(1, 2), (2, 1)])
    relay = [lax.ppermute(h, "src", [(1, 0), (2, 3)]) for h in far]
    pieces = [(0, 0, SPLIT, 0, None), (1, SPLIT, segs - SPLIT, 0, None)]
    out, rows = lags(
        [([(k, 0, segs, 0, None)], at(0)), ([(k + 1, 0, segs, 0, None)], at(1))],
        sources + [whole, near],
        samples,
        n_rcv,
        chans,
        src_slots,
    )
    out = lags([(pieces, at(2))], far, samples, n_rcv, chans, rows=rows, prev=out)
    return lags([(pieces + [(2, 0, segs, 0, inner)], at(3))], relay + [middle], samples, n_rcv, chans, rows=rows, prev=out)


def solution(mesh):
    return jax.shard_map(
        work,
        mesh=mesh,
        in_specs=(
            P(None, ("grp", "rcv", "src"), None),
            P(None, ("grp", "rcv", "src")),
            P(("grp", "rcv", "src"), None),
        ),
        out_specs=P(None, ("grp", "src"), "rcv"),
        check_vma=False,
    )
```

```python
import functools
import math

import ml_dtypes
import numpy as np

import jax
import jax.numpy as jnp
from jax import lax
from jax.experimental import pallas as pl
from jax.experimental.pallas import tpu as pltpu
from jax.sharding import PartitionSpec as P


BINS = 256
LOWBIN = 16
MAXLAG = 32
LAGS = 2 * MAXLAG + 1
BASE = 5
SPACING = 2 * BASE + 1
CENTRES = 7
SPLIT = 5
SRC_DEV = 32
KPARTS = 4


def dft_table(samples):
    t = np.arange(samples, dtype=np.int64)
    k = LOWBIN + np.arange(BINS, dtype=np.int64)
    angle = ((t[:, None] * k[None, :]) % samples) * (2.0 * np.pi / samples)
    taper = (0.5 - 0.5 * np.cos(t * (2.0 * np.pi / samples)))[:, None]
    joined = np.concatenate([taper * np.cos(angle), -taper * np.sin(angle)], axis=1)
    return joined.astype(np.float32).astype(ml_dtypes.bfloat16)


def phase_table(samples, shifts):
    k = LOWBIN + np.arange(BINS, dtype=np.int64)
    angle = ((np.asarray(shifts)[:, None] * k[None, :]) % samples) * (2.0 * np.pi / samples)
    return np.stack([np.cos(angle), np.sin(angle)], axis=1).astype(np.float32)


def spectra_kernel(x_hbm, w_hbm, alive_hbm, picks_hbm, early_ref, late_ref, whole_ref, src_ref, *scratch):
    full, x_buf, w_buf, alive_ref, picks_ref, x_sem, w_sem, small_sem = scratch
    segs, chans, samples = x_hbm.shape
    rows = segs * chans
    step = samples // KPARTS
    split = early_ref.shape[0]
    get_alive = pltpu.make_async_copy(alive_hbm, alive_ref, small_sem.at[0])
    get_picks = pltpu.make_async_copy(picks_hbm, picks_ref, small_sem.at[1])
    get_alive.start()
    get_picks.start()
    copies = []
    for i in range(KPARTS):
        part = pl.ds(i * step, step)
        cx = pltpu.make_async_copy(x_hbm.at[:, :, part], x_buf.at[i], x_sem.at[i])
        cw = pltpu.make_async_copy(w_hbm.at[part, :], w_buf.at[i], w_sem.at[i])
        cx.start()
        cw.start()
        copies.append((cx, cw))
    get_alive.wait()
    get_picks.wait()
    diagonal = lax.broadcasted_iota(jnp.int32, (chans, chans), 0) == lax.broadcasted_iota(jnp.int32, (chans, chans), 1)
    live = []
    for g in range(segs):
        row = jnp.broadcast_to(alive_ref[g : g + 1, :].astype(jnp.float32), (chans, chans))
        live.append(jnp.sum(jnp.where(diagonal, row, 0.0), axis=1, keepdims=True))
    live = jnp.concatenate(live, axis=0)
    total = None
    square = None
    for i in range(KPARTS):
        copies[i][0].wait()
        copies[i][1].wait()
        x = x_buf[i].reshape(rows, step)
        term = jnp.dot(x, w_buf[i], preferred_element_type=jnp.float32)
        xf = x.astype(jnp.float32)
        sq = jnp.sum(xf * xf, axis=1, keepdims=True)
        total = term if total is None else total + term
        square = sq if square is None else square + sq
    mean_square = square * (1.0 / samples)
    weight = live / jnp.sqrt(samples * (mean_square + 1e-06))
    rounded = (total * weight).astype(jnp.bfloat16).reshape(segs, chans, 2 * BINS)
    early_ref[...] = rounded[:split]
    late_ref[...] = rounded[split:]
    whole_ref[...] = rounded
    full[...] = rounded.astype(jnp.float32)
    for j in range(src_ref.shape[1]):
        src_ref[:, j : j + 1, :] = full[:, pl.ds(picks_ref[0, j], 1), :].astype(jnp.bfloat16)


def spectra(traces, alive, picks, pick_count, split):
    segs, chans, samples = traces.shape
    step = samples // KPARTS
    table = jnp.asarray(dft_table(samples))
    vmem, anywhere = pl.BlockSpec(memory_space=pltpu.VMEM), pl.BlockSpec(memory_space=pl.ANY)

    def spec(count, rows=chans):
        return pltpu.VMEM((count, rows, 2 * BINS), jnp.bfloat16)

    return pl.pallas_call(
        spectra_kernel,
        out_shape=(spec(split), spec(segs - split), spec(segs), spec(segs, pick_count)),
        in_specs=[anywhere] * 4,
        out_specs=(vmem,) * 4,
        scratch_shapes=[
            pltpu.VMEM((segs, chans, 2 * BINS), jnp.float32),
            pltpu.VMEM((KPARTS, segs, chans, step), jnp.bfloat16),
            pltpu.VMEM((KPARTS, step, 2 * BINS), jnp.bfloat16),
            pltpu.VMEM(alive.shape, jnp.int32),
            pltpu.SMEM(picks.shape, jnp.int32),
            pltpu.SemaphoreType.DMA((KPARTS,)),
            pltpu.SemaphoreType.DMA((KPARTS,)),
            pltpu.SemaphoreType.DMA((2,)),
        ],
        name="spectra",
    )(traces, table, alive, picks)


def build_rows(tab_ref, sources, src_slots, src_all, rows_ref):
    n_src, width = src_all.shape[1], 2 * BINS
    for piece, slot in zip(sources, src_slots):
        rows = piece.shape[1]
        at = slot() * rows if slot is not None else 0
        src_all[:, pl.ds(at, rows), :] = piece[...].astype(jnp.float32)
    for g in range(src_all.shape[0]):
        a, b = src_all[g, :, :BINS].astype(jnp.bfloat16), src_all[g, :, BINS:].astype(jnp.bfloat16)
        one, two = pl.ds(g * width, BINS), pl.ds(g * width + BINS, BINS)
        for e in range(BASE + 1):
            c = jnp.broadcast_to(tab_ref[e, 0:1, :], (n_src, BINS)).astype(jnp.bfloat16)
            even = pl.ds(e * n_src, n_src)
            rows_ref[even, one] = a * c
            rows_ref[even, two] = b * c
            if e > 0:
                s = jnp.broadcast_to(tab_ref[e, 1:2, :], (n_src, BINS)).astype(jnp.bfloat16)
                odd = pl.ds((BASE + e) * n_src, n_src)
                rows_ref[odd, one] = b * s
                rows_ref[odd, two] = -(a * s)


def build_columns(tab_ref, piece, row, rot):
    width = 2 * BINS
    size = rot.shape[0] // CENTRES
    for g in range(piece.shape[0]):
        both = piece[g, row : row + size, :].astype(jnp.float32)
        p, q = both[:, :BINS], both[:, BINS:]
        one, two = pl.ds(g * width, BINS), pl.ds(g * width + BINS, BINS)

        def keep(centre, real, imag):
            at = pl.ds(centre * size, size)
            rot[at, one] = real.astype(jnp.bfloat16)
            rot[at, two] = imag.astype(jnp.bfloat16)

        keep(0, p, q)
        for i in range(CENTRES // 2):
            c, s = tab_ref[BASE + 1 + i, 0:1, :], tab_ref[BASE + 1 + i, 1:2, :]
            pc, ps, qc, qs = p * c, p * s, q * c, q * s
            keep(2 * i + 1, pc + qs, qc - ps)
            keep(2 * i + 2, pc - qs, qc + ps)


def multiply(tab_ref, pieces, row, rows_ref, rot, start):
    width = 2 * BINS
    total = None
    for piece in pieces:
        count = piece.shape[0]
        here = rot.at[:, pl.ds(start * width, count * width)]
        build_columns(tab_ref, piece, row, here)
        term = lax.dot_general(
            rows_ref[:, pl.ds(start * width, count * width)],
            here[...],
            (((1,), (1,)), ((), ())),
            preferred_element_type=jnp.float32,
        )
        total = term if total is None else total + term
        start += count
    return total


def finish(sums, place, size, n_src, n_rcv, scale, old, out_ref, done=None):
    slots = n_rcv // size
    mine = lax.broadcasted_iota(jnp.int32, (n_src, n_rcv), 1) // size == place

    def put(lag, value, group):
        if 0 <= lag < LAGS:
            moved = (value * scale).astype(jnp.bfloat16)
            if slots > 1:
                moved = pltpu.roll(moved, lax.rem(place - group + slots, slots) * size, 1)
            before = jnp.zeros_like(moved) if old is None else old[lag]
            out_ref[lag] = jnp.where(mine, moved, before)

    order = sorted(range(CENTRES), key=lambda c: ((c + 1) // 2) * (1 if c % 2 else -1))
    for centre in order:
        tile, group = divmod(centre, slots)
        lanes = pl.ds(tile * n_rcv, n_rcv)
        middle = MAXLAG + ((centre + 1) // 2) * SPACING * (1 if centre % 2 else -1)
        for e in range(BASE + 1):
            if not (0 <= middle + e < LAGS or 0 <= middle - e < LAGS):
                continue
            even = sums[pl.ds(e * n_src, n_src), lanes]
            if e == 0:
                put(middle, even, group)
                continue
            odd = sums[pl.ds((BASE + e) * n_src, n_src), lanes]
            put(middle + e, even - odd, group)
            put(middle - e, even + odd, group)
        if done is not None:
            done(max(0, middle - BASE), min(LAGS, middle + BASE + 1))


def own_kernel(slots, src_slots, n_parts, scale, *refs):
    n_in = len(src_slots)
    sources, parts = refs[:n_in], refs[n_in : n_in + n_parts]
    tab_ref, out_ref, rows_ref, rot, sums, src_all = refs[n_in + n_parts :]
    n_src, n_rcv = out_ref.shape[1:]
    size = rot.shape[0] // CENTRES
    build_rows(tab_ref, sources, src_slots, src_all, rows_ref)
    for i, slot in enumerate(slots):
        sums[:, : CENTRES * size] = multiply(tab_ref, parts, i * size, rows_ref, rot, 0)
        finish(sums, slot(), size, n_src, n_rcv, scale, out_ref if i else None, out_ref)


def more_kernel(slots, scale, *refs):
    parts, (tab_ref, rows_ref, prev_ref, out_ref, rot, sums) = refs[:-6], refs[-6:]
    n_src, n_rcv = out_ref.shape[1:]
    size = rot.shape[0] // CENTRES
    each = len(parts) // len(slots)
    for i, slot in enumerate(slots):
        sums[:, : CENTRES * size] = multiply(tab_ref, parts[i * each : (i + 1) * each], 0, rows_ref, rot, 0)
        finish(sums, slot(), size, n_src, n_rcv, scale, out_ref if i else prev_ref, out_ref)


def part_kernel(piece, tab_ref, rows_ref, sums_ref, rot):
    size = rot.shape[0] // CENTRES
    sums_ref[:, : CENTRES * size] = multiply(tab_ref, [piece], 0, rows_ref, rot, 0)


def last_kernel(slot, start, scale, piece, tab_ref, rows_ref, before_ref, prev_ref, out_hbm, rot, sums, out_buf, sem):
    n_src, n_rcv = out_buf.shape[1:]
    size = rot.shape[0] // CENTRES
    used = CENTRES * size
    sums[:, :used] = multiply(tab_ref, [piece], 0, rows_ref, rot, start) + before_ref[:, :used]
    copies = []

    def done(low, high):
        copies.append(pltpu.make_async_copy(out_buf.at[low:high], out_hbm.at[low:high], sem.at[len(copies)]))
        copies[-1].start()

    finish(sums, slot(), size, n_src, n_rcv, scale, prev_ref, out_buf, done)
    for copy in copies:
        copy.wait()


class Lags:
    def __init__(self, segs, samples, n_rcv, size):
        lagged = list(range(BASE + 1)) + [SPACING * i for i in range(1, CENTRES // 2 + 1)]
        self.tab = jnp.asarray(phase_table(samples, lagged))
        self.segs, self.n_rcv, self.size = segs, n_rcv, size
        self.scale = 1.0 / math.sqrt(segs * BINS)
        self.rows = pltpu.VMEM(((2 * BASE + 1) * SRC_DEV, segs * 2 * BINS), jnp.bfloat16)
        self.out = (LAGS, SRC_DEV, n_rcv)
        self.kept = pltpu.VMEM(self.out, jnp.bfloat16)
        self.rot = pltpu.VMEM((CENTRES * size, segs * 2 * BINS), jnp.bfloat16)
        self.sums = pltpu.VMEM(((2 * BASE + 1) * SRC_DEV, pl.cdiv(CENTRES * size, n_rcv) * n_rcv), jnp.float32)

    def call(self, kernel, out_shape, scratch, *arrays, out_specs=None):
        vmem = pl.BlockSpec(memory_space=pltpu.VMEM)
        if out_specs is None:
            out_specs = jax.tree.map(lambda _: vmem, out_shape)
        return pl.pallas_call(
            kernel,
            out_shape=out_shape,
            in_specs=[vmem] * len(arrays),
            out_specs=out_specs,
            scratch_shapes=scratch,
            compiler_params=pltpu.CompilerParams(vmem_limit_bytes=32 << 20),
        )(*arrays)

    def own(self, slots, src_slots, sources, parts, keep=True):
        kernel = functools.partial(own_kernel, slots, src_slots, len(parts), self.scale)
        wide = pltpu.VMEM((self.segs, SRC_DEV, 2 * BINS), jnp.float32)
        out = self.kept if keep else jax.ShapeDtypeStruct(self.out, jnp.bfloat16)
        return self.call(kernel, (out, self.rows), [self.rot, self.sums, wide], *sources, *parts, self.tab)

    def more(self, slots, parts, rows, prev):
        kernel = functools.partial(more_kernel, slots, self.scale)
        return self.call(kernel, self.kept, [self.rot, self.sums], *parts, self.tab, rows, prev)

    def part(self, piece, rows):
        return self.call(part_kernel, self.sums, [self.rot], piece, self.tab, rows)

    def last(self, slot, start, piece, rows, before, prev):
        kernel = functools.partial(last_kernel, slot, start, self.scale)
        out = jax.ShapeDtypeStruct(self.out, jnp.bfloat16)
        scratch = [self.rot, self.sums, self.kept, pltpu.SemaphoreType.DMA((CENTRES,))]
        spec = pl.BlockSpec(memory_space=pl.ANY)
        return self.call(kernel, out, scratch, piece, self.tab, rows, before, prev, out_specs=spec)


def gather_sources(x):
    n = lax.axis_size("rcv")
    if n != 4:
        return [lax.all_gather(x, "rcv", axis=1, tiled=True)], [None]
    moved = [lax.ppermute(x, "rcv", [(i, i ^ k) for i in range(n)]) for k in range(1, n)]
    return [x] + moved, [lambda k=k: lax.axis_index("rcv") ^ k for k in range(n)]


def work(traces, alive, picks):
    segs, chans, samples = traces.shape
    n = lax.axis_size("src")
    n_rcv = n * chans
    early, late, whole, chosen = spectra(traces, alive, picks, SRC_DEV // lax.axis_size("rcv"), SPLIT)
    sources, src_slots = gather_sources(chosen)
    if n != 4:
        panel = lax.all_gather(whole, "src", axis=1, tiled=True)
        slots = [lambda i=i: i for i in range(4)]
        return Lags(segs, samples, n_rcv, n_rcv // 4).own(slots, src_slots, sources, [panel], keep=False)[0]

    def swap(parts, j):
        return [lax.ppermute(h, "src", [(i, i ^ j) for i in range(n)]) for h in parts]

    def slot(j):
        return lambda: lax.axis_index("src") ^ j

    far = swap([early, late], 2)
    near = swap([whole], 1)[0]
    last = swap(far, 1)
    job = Lags(segs, samples, n_rcv, chans)
    out, rows = job.own([slot(0)], src_slots, sources, [whole])
    out = job.more([slot(1)], [near], rows, out)
    out = job.more([slot(2)], far, rows, out)
    before = job.part(last[0], rows)
    return job.last(slot(3), SPLIT, last[1], rows, before, out)


def solution(mesh):
    return jax.shard_map(
        work,
        mesh=mesh,
        in_specs=(
            P(None, ("grp", "rcv", "src"), None),
            P(None, ("grp", "rcv", "src")),
            P(("grp", "rcv", "src"), None),
        ),
        out_specs=P(None, ("grp", "src"), "rcv"),
        check_vma=False,
    )
```

```python
import functools
import math

import ml_dtypes
import numpy as np

import jax
import jax.numpy as jnp
from jax import lax
from jax.experimental import pallas as pl
from jax.experimental.pallas import tpu as pltpu
from jax.sharding import PartitionSpec as P


BINS = 256
LOWBIN = 16
MAXLAG = 32
LAGS = 2 * MAXLAG + 1
BASE = 5
SPACING = 2 * BASE + 1
CENTRES = 7
SPLIT = 5
SRC_DEV = 32
KPARTS = 2


def bin_order():
    k = LOWBIN + np.arange(BINS, dtype=np.int64)
    return k[np.argsort(k % 2, kind="stable")]


def dft_table(samples):
    t = np.arange(samples // 2, dtype=np.int64)
    parts = []
    for k in np.split(bin_order(), 2):
        angle = ((t[:, None] * k[None, :]) % samples) * (2.0 * np.pi / samples)
        parts += [np.cos(angle), -np.sin(angle)]
    return np.concatenate(parts, axis=1).astype(np.float32).astype(ml_dtypes.bfloat16)


def taper_table(samples):
    t = np.arange(samples, dtype=np.int64)
    return (0.5 - 0.5 * np.cos(t * (2.0 * np.pi / samples))).astype(np.float32).reshape(2, samples // 2)


def phase_table(samples, shifts):
    k = bin_order()
    angle = ((np.asarray(shifts)[:, None] * k[None, :]) % samples) * (2.0 * np.pi / samples)
    return np.stack([np.cos(angle), np.sin(angle)], axis=1).astype(np.float32)


def spectra_kernel(x_hbm, w_hbm, taper_hbm, alive_hbm, picks_hbm, early_ref, late_ref, whole_ref, src_ref, *scratch):
    full, x_buf, w_buf, taper_ref, alive_ref, picks_ref, x_sem, w_sem, small_sem = scratch
    segs, chans, samples = x_hbm.shape
    rows = segs * chans
    step = samples // 2 // KPARTS
    split = early_ref.shape[0]
    small = [(alive_hbm, alive_ref), (picks_hbm, picks_ref), (taper_hbm, taper_ref)]
    small = [pltpu.make_async_copy(a, b, small_sem.at[i]) for i, (a, b) in enumerate(small)]
    for copy in small:
        copy.start()
    copies = []
    for i in range(KPARTS):
        group = [pltpu.make_async_copy(w_hbm.at[pl.ds(i * step, step), :], w_buf.at[i], w_sem.at[i])]
        for h in range(2):
            part = pl.ds(h * (samples // 2) + i * step, step)
            group.append(pltpu.make_async_copy(x_hbm.at[:, :, part], x_buf.at[i, h], x_sem.at[i, h]))
        for copy in group:
            copy.start()
        copies.append(group)
    for copy in small:
        copy.wait()
    diagonal = lax.broadcasted_iota(jnp.int32, (chans, chans), 0) == lax.broadcasted_iota(jnp.int32, (chans, chans), 1)
    live = []
    for g in range(segs):
        row = jnp.broadcast_to(alive_ref[g : g + 1, :].astype(jnp.float32), (chans, chans))
        live.append(jnp.sum(jnp.where(diagonal, row, 0.0), axis=1, keepdims=True))
    live = jnp.concatenate(live, axis=0)
    even = odd = square = None
    for i in range(KPARTS):
        for copy in copies[i]:
            copy.wait()
        at = pl.ds(i * step, step)
        low = x_buf[i, 0].reshape(rows, step).astype(jnp.float32)
        high = x_buf[i, 1].reshape(rows, step).astype(jnp.float32)
        sq = jnp.sum(low * low + high * high, axis=1, keepdims=True)
        low, high = low * taper_ref[0:1, at], high * taper_ref[1:2, at]
        both = (low + high).astype(jnp.bfloat16), (low - high).astype(jnp.bfloat16)
        terms = [
            jnp.dot(v, w_buf[i, :, h * BINS : (h + 1) * BINS], preferred_element_type=jnp.float32) for h, v in enumerate(both)
        ]
        even = terms[0] if even is None else even + terms[0]
        odd = terms[1] if odd is None else odd + terms[1]
        square = sq if square is None else square + sq
    half = BINS // 2
    total = jnp.concatenate([even[:, :half], odd[:, :half], even[:, half:], odd[:, half:]], axis=1)
    mean_square = square * (1.0 / samples)
    weight = live / jnp.sqrt(samples * (mean_square + 1e-06))
    rounded = (total * weight).astype(jnp.bfloat16).reshape(segs, chans, 2 * BINS)
    early_ref[...] = rounded[:split]
    late_ref[...] = rounded[split:]
    whole_ref[...] = rounded
    full[...] = rounded.astype(jnp.float32)
    for j in range(src_ref.shape[1]):
        src_ref[:, j : j + 1, :] = full[:, pl.ds(picks_ref[0, j], 1), :].astype(jnp.bfloat16)


def spectra(traces, alive, picks, pick_count, split):
    segs, chans, samples = traces.shape
    step = samples // 2 // KPARTS
    table = jnp.asarray(dft_table(samples))
    vmem, anywhere = pl.BlockSpec(memory_space=pltpu.VMEM), pl.BlockSpec(memory_space=pl.ANY)

    def spec(count, rows=chans):
        return pltpu.VMEM((count, rows, 2 * BINS), jnp.bfloat16)

    return pl.pallas_call(
        spectra_kernel,
        out_shape=(spec(split), spec(segs - split), spec(segs), spec(segs, pick_count)),
        in_specs=[anywhere] * 5,
        out_specs=(vmem,) * 4,
        scratch_shapes=[
            pltpu.VMEM((segs, chans, 2 * BINS), jnp.float32),
            pltpu.VMEM((KPARTS, 2, segs, chans, step), jnp.bfloat16),
            pltpu.VMEM((KPARTS, step, 2 * BINS), jnp.bfloat16),
            pltpu.VMEM((2, samples // 2), jnp.float32),
            pltpu.VMEM(alive.shape, jnp.int32),
            pltpu.SMEM(picks.shape, jnp.int32),
            pltpu.SemaphoreType.DMA((KPARTS, 2)),
            pltpu.SemaphoreType.DMA((KPARTS,)),
            pltpu.SemaphoreType.DMA((3,)),
        ],
        name="spectra",
    )(traces, table, jnp.asarray(taper_table(samples)), alive, picks)


def build_rows(tab_ref, sources, src_slots, src_all, rows_ref):
    n_src, width = src_all.shape[1], 2 * BINS
    for piece, slot in zip(sources, src_slots):
        rows = piece.shape[1]
        at = slot() * rows if slot is not None else 0
        src_all[:, pl.ds(at, rows), :] = piece[...].astype(jnp.float32)
    for g in range(src_all.shape[0]):
        a, b = src_all[g, :, :BINS].astype(jnp.bfloat16), src_all[g, :, BINS:].astype(jnp.bfloat16)
        one, two = pl.ds(g * width, BINS), pl.ds(g * width + BINS, BINS)
        for e in range(BASE + 1):
            c = jnp.broadcast_to(tab_ref[e, 0:1, :], (n_src, BINS)).astype(jnp.bfloat16)
            even = pl.ds(e * n_src, n_src)
            rows_ref[even, one] = a * c
            rows_ref[even, two] = b * c
            if e > 0:
                s = jnp.broadcast_to(tab_ref[e, 1:2, :], (n_src, BINS)).astype(jnp.bfloat16)
                odd = pl.ds((BASE + e) * n_src, n_src)
                rows_ref[odd, one] = b * s
                rows_ref[odd, two] = -(a * s)


def build_columns(tab_ref, piece, row, rot):
    width = 2 * BINS
    size = rot.shape[0] // CENTRES
    for g in range(piece.shape[0]):
        both = piece[g, row : row + size, :].astype(jnp.float32)
        p, q = both[:, :BINS], both[:, BINS:]
        one, two = pl.ds(g * width, BINS), pl.ds(g * width + BINS, BINS)

        def keep(centre, real, imag):
            at = pl.ds(centre * size, size)
            rot[at, one] = real.astype(jnp.bfloat16)
            rot[at, two] = imag.astype(jnp.bfloat16)

        keep(0, p, q)
        for i in range(CENTRES // 2):
            c, s = tab_ref[BASE + 1 + i, 0:1, :], tab_ref[BASE + 1 + i, 1:2, :]
            pc, ps, qc, qs = p * c, p * s, q * c, q * s
            keep(2 * i + 1, pc + qs, qc - ps)
            keep(2 * i + 2, pc - qs, qc + ps)


def multiply(tab_ref, pieces, row, rows_ref, rot, start):
    width = 2 * BINS
    total = None
    for piece in pieces:
        count = piece.shape[0]
        here = rot.at[:, pl.ds(start * width, count * width)]
        build_columns(tab_ref, piece, row, here)
        term = lax.dot_general(
            rows_ref[:, pl.ds(start * width, count * width)],
            here[...],
            (((1,), (1,)), ((), ())),
            preferred_element_type=jnp.float32,
        )
        total = term if total is None else total + term
        start += count
    return total


def finish(sums, place, size, n_src, n_rcv, scale, old, out_ref, done=None):
    slots = n_rcv // size
    mine = lax.broadcasted_iota(jnp.int32, (n_src, n_rcv), 1) // size == place

    def put(lag, value, group):
        if 0 <= lag < LAGS:
            moved = (value * scale).astype(jnp.bfloat16)
            if slots > 1:
                moved = pltpu.roll(moved, lax.rem(place - group + slots, slots) * size, 1)
            before = jnp.zeros_like(moved) if old is None else old[lag]
            out_ref[lag] = jnp.where(mine, moved, before)

    order = sorted(range(CENTRES), key=lambda c: ((c + 1) // 2) * (1 if c % 2 else -1))
    for centre in order:
        tile, group = divmod(centre, slots)
        lanes = pl.ds(tile * n_rcv, n_rcv)
        middle = MAXLAG + ((centre + 1) // 2) * SPACING * (1 if centre % 2 else -1)
        for e in range(BASE + 1):
            if not (0 <= middle + e < LAGS or 0 <= middle - e < LAGS):
                continue
            even = sums[pl.ds(e * n_src, n_src), lanes]
            if e == 0:
                put(middle, even, group)
                continue
            odd = sums[pl.ds((BASE + e) * n_src, n_src), lanes]
            put(middle + e, even - odd, group)
            put(middle - e, even + odd, group)
        if done is not None:
            done(max(0, middle - BASE), min(LAGS, middle + BASE + 1))


def own_kernel(slots, src_slots, n_parts, scale, *refs):
    n_in = len(src_slots)
    sources, parts = refs[:n_in], refs[n_in : n_in + n_parts]
    tab_ref, out_ref, rows_ref, rot, sums, src_all = refs[n_in + n_parts :]
    n_src, n_rcv = out_ref.shape[1:]
    size = rot.shape[0] // CENTRES
    build_rows(tab_ref, sources, src_slots, src_all, rows_ref)
    for i, slot in enumerate(slots):
        sums[:, : CENTRES * size] = multiply(tab_ref, parts, i * size, rows_ref, rot, 0)
        finish(sums, slot(), size, n_src, n_rcv, scale, out_ref if i else None, out_ref)


def more_kernel(slots, scale, *refs):
    parts, (tab_ref, rows_ref, prev_ref, out_ref, rot, sums) = refs[:-6], refs[-6:]
    n_src, n_rcv = out_ref.shape[1:]
    size = rot.shape[0] // CENTRES
    each = len(parts) // len(slots)
    for i, slot in enumerate(slots):
        sums[:, : CENTRES * size] = multiply(tab_ref, parts[i * each : (i + 1) * each], 0, rows_ref, rot, 0)
        finish(sums, slot(), size, n_src, n_rcv, scale, out_ref if i else prev_ref, out_ref)


def part_kernel(piece, tab_ref, rows_ref, sums_ref, rot):
    size = rot.shape[0] // CENTRES
    sums_ref[:, : CENTRES * size] = multiply(tab_ref, [piece], 0, rows_ref, rot, 0)


def last_kernel(slot, start, scale, piece, tab_ref, rows_ref, before_ref, prev_ref, out_hbm, rot, sums, out_buf, sem):
    n_src, n_rcv = out_buf.shape[1:]
    size = rot.shape[0] // CENTRES
    used = CENTRES * size
    sums[:, :used] = multiply(tab_ref, [piece], 0, rows_ref, rot, start) + before_ref[:, :used]
    copies = []

    def done(low, high):
        copies.append(pltpu.make_async_copy(out_buf.at[low:high], out_hbm.at[low:high], sem.at[len(copies)]))
        copies[-1].start()

    finish(sums, slot(), size, n_src, n_rcv, scale, prev_ref, out_buf, done)
    for copy in copies:
        copy.wait()


class Lags:
    def __init__(self, segs, samples, n_rcv, size):
        lagged = list(range(BASE + 1)) + [SPACING * i for i in range(1, CENTRES // 2 + 1)]
        self.tab = jnp.asarray(phase_table(samples, lagged))
        self.segs, self.n_rcv, self.size = segs, n_rcv, size
        self.scale = 1.0 / math.sqrt(segs * BINS)
        self.rows = pltpu.VMEM(((2 * BASE + 1) * SRC_DEV, segs * 2 * BINS), jnp.bfloat16)
        self.out = (LAGS, SRC_DEV, n_rcv)
        self.kept = pltpu.VMEM(self.out, jnp.bfloat16)
        self.rot = pltpu.VMEM((CENTRES * size, segs * 2 * BINS), jnp.bfloat16)
        self.sums = pltpu.VMEM(((2 * BASE + 1) * SRC_DEV, pl.cdiv(CENTRES * size, n_rcv) * n_rcv), jnp.float32)

    def call(self, kernel, out_shape, scratch, *arrays, out_specs=None):
        vmem = pl.BlockSpec(memory_space=pltpu.VMEM)
        if out_specs is None:
            out_specs = jax.tree.map(lambda _: vmem, out_shape)
        return pl.pallas_call(
            kernel,
            out_shape=out_shape,
            in_specs=[vmem] * len(arrays),
            out_specs=out_specs,
            scratch_shapes=scratch,
            compiler_params=pltpu.CompilerParams(vmem_limit_bytes=32 << 20),
        )(*arrays)

    def own(self, slots, src_slots, sources, parts, keep=True):
        kernel = functools.partial(own_kernel, slots, src_slots, len(parts), self.scale)
        wide = pltpu.VMEM((self.segs, SRC_DEV, 2 * BINS), jnp.float32)
        out = self.kept if keep else jax.ShapeDtypeStruct(self.out, jnp.bfloat16)
        return self.call(kernel, (out, self.rows), [self.rot, self.sums, wide], *sources, *parts, self.tab)

    def more(self, slots, parts, rows, prev):
        kernel = functools.partial(more_kernel, slots, self.scale)
        return self.call(kernel, self.kept, [self.rot, self.sums], *parts, self.tab, rows, prev)

    def part(self, piece, rows):
        return self.call(part_kernel, self.sums, [self.rot], piece, self.tab, rows)

    def last(self, slot, start, piece, rows, before, prev):
        kernel = functools.partial(last_kernel, slot, start, self.scale)
        out = jax.ShapeDtypeStruct(self.out, jnp.bfloat16)
        scratch = [self.rot, self.sums, self.kept, pltpu.SemaphoreType.DMA((CENTRES,))]
        spec = pl.BlockSpec(memory_space=pl.ANY)
        return self.call(kernel, out, scratch, piece, self.tab, rows, before, prev, out_specs=spec)


def gather_sources(x):
    n = lax.axis_size("rcv")
    if n != 4:
        return [lax.all_gather(x, "rcv", axis=1, tiled=True)], [None]
    moved = [lax.ppermute(x, "rcv", [(i, i ^ k) for i in range(n)]) for k in range(1, n)]
    return [x] + moved, [lambda k=k: lax.axis_index("rcv") ^ k for k in range(n)]


def work(traces, alive, picks):
    segs, chans, samples = traces.shape
    n = lax.axis_size("src")
    n_rcv = n * chans
    early, late, whole, chosen = spectra(traces, alive, picks, SRC_DEV // lax.axis_size("rcv"), SPLIT)
    sources, src_slots = gather_sources(chosen)
    if n != 4:
        panel = lax.all_gather(whole, "src", axis=1, tiled=True)
        slots = [lambda i=i: i for i in range(4)]
        return Lags(segs, samples, n_rcv, n_rcv // 4).own(slots, src_slots, sources, [panel], keep=False)[0]

    def swap(parts, j):
        return [lax.ppermute(h, "src", [(i, i ^ j) for i in range(n)]) for h in parts]

    def slot(j):
        return lambda: lax.axis_index("src") ^ j

    far = swap([early, late], 2)
    near = swap([whole], 1)[0]
    last = swap(far, 1)
    job = Lags(segs, samples, n_rcv, chans)
    out, rows = job.own([slot(0)], src_slots, sources, [whole])
    out = job.more([slot(1)], [near], rows, out)
    out = job.more([slot(2)], far, rows, out)
    before = job.part(last[0], rows)
    return job.last(slot(3), SPLIT, last[1], rows, before, out)


def solution(mesh):
    return jax.shard_map(
        work,
        mesh=mesh,
        in_specs=(
            P(None, ("grp", "rcv", "src"), None),
            P(None, ("grp", "rcv", "src")),
            P(("grp", "rcv", "src"), None),
        ),
        out_specs=P(None, ("grp", "src"), "rcv"),
        check_vma=False,
    )
```

```python
import functools
import math

import ml_dtypes
import numpy as np

import jax
import jax.numpy as jnp
from jax import lax
from jax.experimental import pallas as pl
from jax.experimental.pallas import tpu as pltpu
from jax.sharding import PartitionSpec as P


BINS = 256
LOWBIN = 16
MAXLAG = 32
LAGS = 2 * MAXLAG + 1
BASE = 5
SPACING = 2 * BASE + 1
CENTRES = 7
SPLIT = 5
SRC_DEV = 32
KPARTS = 4


def dft_table(samples):
    t = np.arange(samples, dtype=np.int64)
    k = LOWBIN + np.arange(BINS, dtype=np.int64)
    angle = ((t[:, None] * k[None, :]) % samples) * (2.0 * np.pi / samples)
    taper = (0.5 - 0.5 * np.cos(t * (2.0 * np.pi / samples)))[:, None]
    joined = np.concatenate([taper * np.cos(angle), -taper * np.sin(angle)], axis=1)
    return joined.astype(np.float32).astype(ml_dtypes.bfloat16)


def phase_table(samples, shifts):
    k = LOWBIN + np.arange(BINS, dtype=np.int64)
    angle = ((np.asarray(shifts)[:, None] * k[None, :]) % samples) * (2.0 * np.pi / samples)
    return np.stack([np.cos(angle), np.sin(angle)], axis=1).astype(np.float32)


def spectra_kernel(x_hbm, w_hbm, alive_hbm, picks_hbm, early_ref, late_ref, whole_ref, src_ref, *scratch):
    full, x_buf, w_buf, alive_ref, picks_ref, x_sem, w_sem, small_sem = scratch
    segs, chans, samples = x_hbm.shape
    rows = segs * chans
    step = samples // KPARTS
    split = early_ref.shape[0]
    get_alive = pltpu.make_async_copy(alive_hbm, alive_ref, small_sem.at[0])
    get_picks = pltpu.make_async_copy(picks_hbm, picks_ref, small_sem.at[1])
    get_alive.start()
    get_picks.start()
    copies = []
    for i in range(KPARTS):
        part = pl.ds(i * step, step)
        cx = pltpu.make_async_copy(x_hbm.at[:, :, part], x_buf.at[i], x_sem.at[i])
        cw = pltpu.make_async_copy(w_hbm.at[part, :], w_buf.at[i], w_sem.at[i])
        cx.start()
        cw.start()
        copies.append((cx, cw))
    get_alive.wait()
    get_picks.wait()
    diagonal = lax.broadcasted_iota(jnp.int32, (chans, chans), 0) == lax.broadcasted_iota(jnp.int32, (chans, chans), 1)
    live = []
    for g in range(segs):
        row = jnp.broadcast_to(alive_ref[g : g + 1, :].astype(jnp.float32), (chans, chans))
        live.append(jnp.sum(jnp.where(diagonal, row, 0.0), axis=1, keepdims=True))
    live = jnp.concatenate(live, axis=0)
    total = None
    square = None
    for i in range(KPARTS):
        copies[i][0].wait()
        copies[i][1].wait()
        x = x_buf[i].reshape(rows, step)
        term = jnp.dot(x, w_buf[i], preferred_element_type=jnp.float32)
        xf = x.astype(jnp.float32)
        sq = jnp.sum(xf * xf, axis=1, keepdims=True)
        total = term if total is None else total + term
        square = sq if square is None else square + sq
    mean_square = square * (1.0 / samples)
    weight = live / jnp.sqrt(samples * (mean_square + 1e-06))
    rounded = (total * weight).astype(jnp.bfloat16).reshape(segs, chans, 2 * BINS)
    early_ref[...] = rounded[:split]
    late_ref[...] = rounded[split:]
    whole_ref[...] = rounded
    full[...] = rounded.astype(jnp.float32)
    for j in range(src_ref.shape[1]):
        src_ref[:, j : j + 1, :] = full[:, pl.ds(picks_ref[0, j], 1), :].astype(jnp.bfloat16)


def spectra(traces, alive, picks, pick_count, split):
    segs, chans, samples = traces.shape
    step = samples // KPARTS
    table = jnp.asarray(dft_table(samples))
    vmem, anywhere = pl.BlockSpec(memory_space=pltpu.VMEM), pl.BlockSpec(memory_space=pl.ANY)

    def spec(count, rows=chans):
        return pltpu.VMEM((count, rows, 2 * BINS), jnp.bfloat16)

    return pl.pallas_call(
        spectra_kernel,
        out_shape=(spec(split), spec(segs - split), spec(segs), spec(segs, pick_count)),
        in_specs=[anywhere] * 4,
        out_specs=(vmem,) * 4,
        scratch_shapes=[
            pltpu.VMEM((segs, chans, 2 * BINS), jnp.float32),
            pltpu.VMEM((KPARTS, segs, chans, step), jnp.bfloat16),
            pltpu.VMEM((KPARTS, step, 2 * BINS), jnp.bfloat16),
            pltpu.VMEM(alive.shape, jnp.int32),
            pltpu.SMEM(picks.shape, jnp.int32),
            pltpu.SemaphoreType.DMA((KPARTS,)),
            pltpu.SemaphoreType.DMA((KPARTS,)),
            pltpu.SemaphoreType.DMA((2,)),
        ],
        name="spectra",
    )(traces, table, alive, picks)


def build_rows(tab_ref, sources, src_slots, src_all, rows_ref):
    n_src, width = src_all.shape[1], 2 * BINS
    for piece, slot in zip(sources, src_slots):
        rows = piece.shape[1]
        at = slot() * rows if slot is not None else 0
        src_all[:, pl.ds(at, rows), :] = piece[...].astype(jnp.float32)
    for g in range(src_all.shape[0]):
        a, b = src_all[g, :, :BINS].astype(jnp.bfloat16), src_all[g, :, BINS:].astype(jnp.bfloat16)
        one, two = pl.ds(g * width, BINS), pl.ds(g * width + BINS, BINS)
        for e in range(BASE + 1):
            c = jnp.broadcast_to(tab_ref[e, 0:1, :], (n_src, BINS)).astype(jnp.bfloat16)
            even = pl.ds(e * n_src, n_src)
            rows_ref[even, one] = a * c
            rows_ref[even, two] = b * c
            if e > 0:
                s = jnp.broadcast_to(tab_ref[e, 1:2, :], (n_src, BINS)).astype(jnp.bfloat16)
                odd = pl.ds((BASE + e) * n_src, n_src)
                rows_ref[odd, one] = b * s
                rows_ref[odd, two] = -(a * s)


def build_columns(tab_ref, piece, row, rot):
    width = 2 * BINS
    size = rot.shape[0] // CENTRES
    for g in range(piece.shape[0]):
        both = piece[g, row : row + size, :].astype(jnp.float32)
        p, q = both[:, :BINS], both[:, BINS:]
        one, two = pl.ds(g * width, BINS), pl.ds(g * width + BINS, BINS)

        def keep(centre, real, imag):
            at = pl.ds(centre * size, size)
            rot[at, one] = real.astype(jnp.bfloat16)
            rot[at, two] = imag.astype(jnp.bfloat16)

        keep(0, p, q)
        for i in range(CENTRES // 2):
            c, s = tab_ref[BASE + 1 + i, 0:1, :], tab_ref[BASE + 1 + i, 1:2, :]
            pc, ps, qc, qs = p * c, p * s, q * c, q * s
            keep(2 * i + 1, pc + qs, qc - ps)
            keep(2 * i + 2, pc - qs, qc + ps)


def multiply(tab_ref, pieces, row, rows_ref, rot, start):
    width = 2 * BINS
    total = None
    for piece in pieces:
        count = piece.shape[0]
        here = rot.at[:, pl.ds(start * width, count * width)]
        build_columns(tab_ref, piece, row, here)
        term = lax.dot_general(
            rows_ref[:, pl.ds(start * width, count * width)],
            here[...],
            (((1,), (1,)), ((), ())),
            preferred_element_type=jnp.float32,
        )
        total = term if total is None else total + term
        start += count
    return total


def finish(sums, place, size, n_src, n_rcv, scale, old, out_ref, done=None):
    slots = n_rcv // size
    mine = lax.broadcasted_iota(jnp.int32, (n_src, n_rcv), 1) // size == place

    def put(lag, value, group):
        if 0 <= lag < LAGS:
            moved = pltpu.roll(value, lax.rem(place - group + slots, slots) * size, 1) if slots > 1 else value
            before = 0.0 if old is None else old[lag].astype(jnp.float32)
            out_ref[lag] = jnp.where(mine, moved * scale, before).astype(jnp.bfloat16)

    order = sorted(range(CENTRES), key=lambda c: ((c + 1) // 2) * (1 if c % 2 else -1))
    for centre in order:
        tile, group = divmod(centre, slots)
        lanes = pl.ds(tile * n_rcv, n_rcv)
        middle = MAXLAG + ((centre + 1) // 2) * SPACING * (1 if centre % 2 else -1)
        for e in range(BASE + 1):
            if not (0 <= middle + e < LAGS or 0 <= middle - e < LAGS):
                continue
            even = sums[pl.ds(e * n_src, n_src), lanes]
            if e == 0:
                put(middle, even, group)
                continue
            odd = sums[pl.ds((BASE + e) * n_src, n_src), lanes]
            put(middle + e, even - odd, group)
            put(middle - e, even + odd, group)
        if done is not None:
            done(max(0, middle - BASE), min(LAGS, middle + BASE + 1))


def own_kernel(slots, src_slots, n_parts, scale, *refs):
    n_in = len(src_slots)
    sources, parts = refs[:n_in], refs[n_in : n_in + n_parts]
    tab_ref, out_ref, rows_ref, rot, sums, src_all = refs[n_in + n_parts :]
    n_src, n_rcv = out_ref.shape[1:]
    size = rot.shape[0] // CENTRES
    build_rows(tab_ref, sources, src_slots, src_all, rows_ref)
    for i, slot in enumerate(slots):
        sums[:, : CENTRES * size] = multiply(tab_ref, parts, i * size, rows_ref, rot, 0)
        finish(sums, slot(), size, n_src, n_rcv, scale, out_ref if i else None, out_ref)


def more_kernel(slots, scale, *refs):
    parts, (tab_ref, rows_ref, prev_ref, out_ref, rot, sums) = refs[:-6], refs[-6:]
    n_src, n_rcv = out_ref.shape[1:]
    size = rot.shape[0] // CENTRES
    each = len(parts) // len(slots)
    for i, slot in enumerate(slots):
        sums[:, : CENTRES * size] = multiply(tab_ref, parts[i * each : (i + 1) * each], 0, rows_ref, rot, 0)
        finish(sums, slot(), size, n_src, n_rcv, scale, out_ref if i else prev_ref, out_ref)


def part_kernel(piece, tab_ref, rows_ref, sums_ref, rot):
    size = rot.shape[0] // CENTRES
    sums_ref[:, : CENTRES * size] = multiply(tab_ref, [piece], 0, rows_ref, rot, 0)


def last_kernel(slot, start, scale, piece, tab_ref, rows_ref, before_ref, prev_ref, out_hbm, rot, sums, out_buf, sem):
    n_src, n_rcv = out_buf.shape[1:]
    size = rot.shape[0] // CENTRES
    used = CENTRES * size
    sums[:, :used] = multiply(tab_ref, [piece], 0, rows_ref, rot, start) + before_ref[:, :used]
    copies = []

    def done(low, high):
        copies.append(pltpu.make_async_copy(out_buf.at[low:high], out_hbm.at[low:high], sem.at[len(copies)]))
        copies[-1].start()

    finish(sums, slot(), size, n_src, n_rcv, scale, prev_ref, out_buf, done)
    for copy in copies:
        copy.wait()


class Lags:
    def __init__(self, segs, samples, n_rcv, size):
        lagged = list(range(BASE + 1)) + [SPACING * i for i in range(1, CENTRES // 2 + 1)]
        self.tab = jnp.asarray(phase_table(samples, lagged))
        self.segs, self.n_rcv, self.size = segs, n_rcv, size
        self.scale = 1.0 / math.sqrt(segs * BINS)
        self.rows = pltpu.VMEM(((2 * BASE + 1) * SRC_DEV, segs * 2 * BINS), jnp.bfloat16)
        self.out = (LAGS, SRC_DEV, n_rcv)
        self.kept = pltpu.VMEM(self.out, jnp.bfloat16)
        self.rot = pltpu.VMEM((CENTRES * size, segs * 2 * BINS), jnp.bfloat16)
        self.sums = pltpu.VMEM(((2 * BASE + 1) * SRC_DEV, pl.cdiv(CENTRES * size, n_rcv) * n_rcv), jnp.float32)

    def call(self, kernel, out_shape, scratch, *arrays, out_specs=None):
        vmem = pl.BlockSpec(memory_space=pltpu.VMEM)
        if out_specs is None:
            out_specs = jax.tree.map(lambda _: vmem, out_shape)
        return pl.pallas_call(
            kernel,
            out_shape=out_shape,
            in_specs=[vmem] * len(arrays),
            out_specs=out_specs,
            scratch_shapes=scratch,
            compiler_params=pltpu.CompilerParams(vmem_limit_bytes=32 << 20),
        )(*arrays)

    def own(self, slots, src_slots, sources, parts, keep=True):
        kernel = functools.partial(own_kernel, slots, src_slots, len(parts), self.scale)
        wide = pltpu.VMEM((self.segs, SRC_DEV, 2 * BINS), jnp.float32)
        out = self.kept if keep else jax.ShapeDtypeStruct(self.out, jnp.bfloat16)
        return self.call(kernel, (out, self.rows), [self.rot, self.sums, wide], *sources, *parts, self.tab)

    def more(self, slots, parts, rows, prev):
        kernel = functools.partial(more_kernel, slots, self.scale)
        return self.call(kernel, self.kept, [self.rot, self.sums], *parts, self.tab, rows, prev)

    def part(self, piece, rows):
        return self.call(part_kernel, self.sums, [self.rot], piece, self.tab, rows)

    def last(self, slot, start, piece, rows, before, prev):
        kernel = functools.partial(last_kernel, slot, start, self.scale)
        out = jax.ShapeDtypeStruct(self.out, jnp.bfloat16)
        scratch = [self.rot, self.sums, self.kept, pltpu.SemaphoreType.DMA((CENTRES,))]
        spec = pl.BlockSpec(memory_space=pl.ANY)
        return self.call(kernel, out, scratch, piece, self.tab, rows, before, prev, out_specs=spec)


def gather_sources(x):
    n = lax.axis_size("rcv")
    if n != 4:
        return [lax.all_gather(x, "rcv", axis=1, tiled=True)], [None]
    moved = [lax.ppermute(x, "rcv", [(i, i ^ k) for i in range(n)]) for k in range(1, n)]
    return [x] + moved, [lambda k=k: lax.axis_index("rcv") ^ k for k in range(n)]


def work(traces, alive, picks):
    segs, chans, samples = traces.shape
    n = lax.axis_size("src")
    n_rcv = n * chans
    early, late, whole, chosen = spectra(traces, alive, picks, SRC_DEV // lax.axis_size("rcv"), SPLIT)
    sources, src_slots = gather_sources(chosen)
    if n != 4:
        panel = lax.all_gather(whole, "src", axis=1, tiled=True)
        slots = [lambda i=i: i for i in range(4)]
        return Lags(segs, samples, n_rcv, n_rcv // 4).own(slots, src_slots, sources, [panel], keep=False)[0]

    def swap(parts, j):
        return [lax.ppermute(h, "src", [(i, i ^ j) for i in range(n)]) for h in parts]

    def slot(j):
        return lambda: lax.axis_index("src") ^ j

    far = swap([early, late], 2)
    near = swap([whole], 1)[0]
    last = swap(far, 1)
    job = Lags(segs, samples, n_rcv, chans)
    out, rows = job.own([slot(0)], src_slots, sources, [whole])
    out = job.more([slot(1)], [near], rows, out)
    out = job.more([slot(2)], far, rows, out)
    before = job.part(last[0], rows)
    return job.last(slot(3), SPLIT, last[1], rows, before, out)


def solution(mesh):
    return jax.shard_map(
        work,
        mesh=mesh,
        in_specs=(
            P(None, ("grp", "rcv", "src"), None),
            P(None, ("grp", "rcv", "src")),
            P(("grp", "rcv", "src"), None),
        ),
        out_specs=P(None, ("grp", "src"), "rcv"),
        check_vma=False,
    )
```

```python
import functools
import math

import ml_dtypes
import numpy as np

import jax
import jax.numpy as jnp
from jax import lax
from jax.experimental import pallas as pl
from jax.experimental.pallas import tpu as pltpu
from jax.sharding import PartitionSpec as P


BINS = 256
LOWBIN = 16
MAXLAG = 32
LAGS = 2 * MAXLAG + 1
BASE = 5
SPACING = 2 * BASE + 1
CENTRES = 7
SPLIT = 4
SRC_DEV = 32
KPARTS = 4


def dft_table(samples):
    t = np.arange(samples, dtype=np.int64)
    k = LOWBIN + np.arange(BINS, dtype=np.int64)
    angle = ((t[:, None] * k[None, :]) % samples) * (2.0 * np.pi / samples)
    taper = (0.5 - 0.5 * np.cos(t * (2.0 * np.pi / samples)))[:, None]
    joined = np.concatenate([taper * np.cos(angle), -taper * np.sin(angle)], axis=1)
    return joined.astype(np.float32).astype(ml_dtypes.bfloat16)


def phase_table(samples, shifts):
    k = LOWBIN + np.arange(BINS, dtype=np.int64)
    angle = ((np.asarray(shifts)[:, None] * k[None, :]) % samples) * (2.0 * np.pi / samples)
    return np.stack([np.cos(angle), np.sin(angle)], axis=1).astype(np.float32)


def spectra_kernel(x_hbm, w_hbm, alive_ref, picks_ref, early_ref, late_ref, whole_ref, src_ref, full, x_buf, w_buf, x_sem, w_sem):
    segs, chans, samples = x_hbm.shape
    rows = segs * chans
    step = samples // KPARTS
    split = early_ref.shape[0]
    copies = []
    for i in range(KPARTS):
        part = pl.ds(i * step, step)
        cx = pltpu.make_async_copy(x_hbm.at[:, :, part], x_buf.at[i], x_sem.at[i])
        cw = pltpu.make_async_copy(w_hbm.at[part, :], w_buf.at[i], w_sem.at[i])
        cx.start()
        cw.start()
        copies.append((cx, cw))
    diagonal = lax.broadcasted_iota(jnp.int32, (chans, chans), 0) == lax.broadcasted_iota(jnp.int32, (chans, chans), 1)
    live = []
    for g in range(segs):
        row = jnp.broadcast_to(alive_ref[g : g + 1, :].astype(jnp.float32), (chans, chans))
        live.append(jnp.sum(jnp.where(diagonal, row, 0.0), axis=1, keepdims=True))
    live = jnp.concatenate(live, axis=0)
    total = None
    square = None
    for i in range(KPARTS):
        copies[i][0].wait()
        copies[i][1].wait()
        x = x_buf[i].reshape(rows, step)
        term = jnp.dot(x, w_buf[i], preferred_element_type=jnp.float32)
        xf = x.astype(jnp.float32)
        sq = jnp.sum(xf * xf, axis=1, keepdims=True)
        total = term if total is None else total + term
        square = sq if square is None else square + sq
    mean_square = square * (1.0 / samples)
    weight = live / jnp.sqrt(samples * (mean_square + 1e-06))
    rounded = (total * weight).astype(jnp.bfloat16).reshape(segs, chans, 2 * BINS)
    early_ref[...] = rounded[:split]
    late_ref[...] = rounded[split:]
    whole_ref[...] = rounded
    full[...] = rounded.astype(jnp.float32)
    for j in range(src_ref.shape[1]):
        src_ref[:, j : j + 1, :] = full[:, pl.ds(picks_ref[0, j], 1), :].astype(jnp.bfloat16)


def spectra(traces, alive, picks, pick_count, split):
    segs, chans, samples = traces.shape
    step = samples // KPARTS
    table = jnp.asarray(dft_table(samples))
    vmem, anywhere = pl.BlockSpec(memory_space=pltpu.VMEM), pl.BlockSpec(memory_space=pl.ANY)

    def spec(count, rows=chans):
        return pltpu.VMEM((count, rows, 2 * BINS), jnp.bfloat16)

    return pl.pallas_call(
        spectra_kernel,
        out_shape=(spec(split), spec(segs - split), spec(segs), spec(segs, pick_count)),
        in_specs=[anywhere, anywhere, vmem, pl.BlockSpec(memory_space=pltpu.SMEM)],
        out_specs=(vmem,) * 4,
        scratch_shapes=[
            pltpu.VMEM((segs, chans, 2 * BINS), jnp.float32),
            pltpu.VMEM((KPARTS, segs, chans, step), jnp.bfloat16),
            pltpu.VMEM((KPARTS, step, 2 * BINS), jnp.bfloat16),
            pltpu.SemaphoreType.DMA((KPARTS,)),
            pltpu.SemaphoreType.DMA((KPARTS,)),
        ],
        name="spectra",
    )(traces, table, alive, picks)


def build_rows(tab_ref, sources, src_slots, src_all, rows_ref):
    n_src, width = src_all.shape[1], 2 * BINS
    for piece, slot in zip(sources, src_slots):
        rows = piece.shape[1]
        at = slot() * rows if slot is not None else 0
        src_all[:, pl.ds(at, rows), :] = piece[...].astype(jnp.float32)
    for g in range(src_all.shape[0]):
        a, b = src_all[g, :, :BINS].astype(jnp.bfloat16), src_all[g, :, BINS:].astype(jnp.bfloat16)
        one, two = pl.ds(g * width, BINS), pl.ds(g * width + BINS, BINS)
        for e in range(BASE + 1):
            c = jnp.broadcast_to(tab_ref[e, 0:1, :], (n_src, BINS)).astype(jnp.bfloat16)
            even = pl.ds(e * n_src, n_src)
            rows_ref[even, one] = a * c
            rows_ref[even, two] = b * c
            if e > 0:
                s = jnp.broadcast_to(tab_ref[e, 1:2, :], (n_src, BINS)).astype(jnp.bfloat16)
                odd = pl.ds((BASE + e) * n_src, n_src)
                rows_ref[odd, one] = b * s
                rows_ref[odd, two] = -(a * s)


def build_columns(tab_ref, piece, row, rot):
    width = 2 * BINS
    size = rot.shape[0] // CENTRES
    for g in range(piece.shape[0]):
        both = piece[g, row : row + size, :].astype(jnp.float32)
        p, q = both[:, :BINS], both[:, BINS:]
        one, two = pl.ds(g * width, BINS), pl.ds(g * width + BINS, BINS)

        def keep(centre, real, imag):
            at = pl.ds(centre * size, size)
            rot[at, one] = real.astype(jnp.bfloat16)
            rot[at, two] = imag.astype(jnp.bfloat16)

        keep(0, p, q)
        for i in range(CENTRES // 2):
            c, s = tab_ref[BASE + 1 + i, 0:1, :], tab_ref[BASE + 1 + i, 1:2, :]
            pc, ps, qc, qs = p * c, p * s, q * c, q * s
            keep(2 * i + 1, pc + qs, qc - ps)
            keep(2 * i + 2, pc - qs, qc + ps)


def multiply(tab_ref, pieces, row, rows_ref, rot, start):
    width = 2 * BINS
    total = None
    for piece in pieces:
        count = piece.shape[0]
        here = rot.at[:, pl.ds(start * width, count * width)]
        build_columns(tab_ref, piece, row, here)
        term = lax.dot_general(
            rows_ref[:, pl.ds(start * width, count * width)],
            here[...],
            (((1,), (1,)), ((), ())),
            preferred_element_type=jnp.float32,
        )
        total = term if total is None else total + term
        start += count
    return total


def finish(sums, place, size, n_src, n_rcv, scale, old, out_ref, done=None):
    slots = n_rcv // size
    mine = lax.broadcasted_iota(jnp.int32, (n_src, n_rcv), 1) // size == place

    def put(lag, value, group):
        if 0 <= lag < LAGS:
            moved = pltpu.roll(value, lax.rem(place - group + slots, slots) * size, 1) if slots > 1 else value
            before = 0.0 if old is None else old[lag].astype(jnp.float32)
            out_ref[lag] = jnp.where(mine, moved * scale, before).astype(jnp.bfloat16)

    order = sorted(range(CENTRES), key=lambda c: ((c + 1) // 2) * (1 if c % 2 else -1))
    for centre in order:
        tile, group = divmod(centre, slots)
        lanes = pl.ds(tile * n_rcv, n_rcv)
        middle = MAXLAG + ((centre + 1) // 2) * SPACING * (1 if centre % 2 else -1)
        for e in range(BASE + 1):
            if not (0 <= middle + e < LAGS or 0 <= middle - e < LAGS):
                continue
            even = sums[pl.ds(e * n_src, n_src), lanes]
            if e == 0:
                put(middle, even, group)
                continue
            odd = sums[pl.ds((BASE + e) * n_src, n_src), lanes]
            put(middle + e, even - odd, group)
            put(middle - e, even + odd, group)
        if done is not None:
            done(max(0, middle - BASE), min(LAGS, middle + BASE + 1))


def own_kernel(slots, src_slots, n_parts, scale, *refs):
    n_in = len(src_slots)
    sources, parts = refs[:n_in], refs[n_in : n_in + n_parts]
    tab_ref, out_ref, rows_ref, rot, sums, src_all = refs[n_in + n_parts :]
    n_src, n_rcv = out_ref.shape[1:]
    size = rot.shape[0] // CENTRES
    build_rows(tab_ref, sources, src_slots, src_all, rows_ref)
    for i, slot in enumerate(slots):
        sums[:, : CENTRES * size] = multiply(tab_ref, parts, i * size, rows_ref, rot, 0)
        finish(sums, slot(), size, n_src, n_rcv, scale, out_ref if i else None, out_ref)


def more_kernel(slots, scale, *refs):
    parts, (tab_ref, rows_ref, prev_ref, out_ref, rot, sums) = refs[:-6], refs[-6:]
    n_src, n_rcv = out_ref.shape[1:]
    size = rot.shape[0] // CENTRES
    each = len(parts) // len(slots)
    for i, slot in enumerate(slots):
        sums[:, : CENTRES * size] = multiply(tab_ref, parts[i * each : (i + 1) * each], 0, rows_ref, rot, 0)
        finish(sums, slot(), size, n_src, n_rcv, scale, out_ref if i else prev_ref, out_ref)


def part_kernel(piece, tab_ref, rows_ref, sums_ref, rot):
    size = rot.shape[0] // CENTRES
    sums_ref[:, : CENTRES * size] = multiply(tab_ref, [piece], 0, rows_ref, rot, 0)


def last_kernel(slot, start, scale, piece, tab_ref, rows_ref, before_ref, prev_ref, out_hbm, rot, sums, out_buf, sem):
    n_src, n_rcv = out_buf.shape[1:]
    size = rot.shape[0] // CENTRES
    used = CENTRES * size
    sums[:, :used] = multiply(tab_ref, [piece], 0, rows_ref, rot, start) + before_ref[:, :used]
    copies = []

    def done(low, high):
        copies.append(pltpu.make_async_copy(out_buf.at[low:high], out_hbm.at[low:high], sem.at[len(copies)]))
        copies[-1].start()

    finish(sums, slot(), size, n_src, n_rcv, scale, prev_ref, out_buf, done)
    for copy in copies:
        copy.wait()


class Lags:
    def __init__(self, segs, samples, n_rcv, size):
        lagged = list(range(BASE + 1)) + [SPACING * i for i in range(1, CENTRES // 2 + 1)]
        self.tab = jnp.asarray(phase_table(samples, lagged))
        self.segs, self.n_rcv, self.size = segs, n_rcv, size
        self.scale = 1.0 / math.sqrt(segs * BINS)
        self.rows = pltpu.VMEM(((2 * BASE + 1) * SRC_DEV, segs * 2 * BINS), jnp.bfloat16)
        self.out = (LAGS, SRC_DEV, n_rcv)
        self.kept = pltpu.VMEM(self.out, jnp.bfloat16)
        self.rot = pltpu.VMEM((CENTRES * size, segs * 2 * BINS), jnp.bfloat16)
        self.sums = pltpu.VMEM(((2 * BASE + 1) * SRC_DEV, pl.cdiv(CENTRES * size, n_rcv) * n_rcv), jnp.float32)

    def call(self, kernel, out_shape, scratch, *arrays, out_specs=None):
        vmem = pl.BlockSpec(memory_space=pltpu.VMEM)
        if out_specs is None:
            out_specs = jax.tree.map(lambda _: vmem, out_shape)
        return pl.pallas_call(
            kernel,
            out_shape=out_shape,
            in_specs=[vmem] * len(arrays),
            out_specs=out_specs,
            scratch_shapes=scratch,
            compiler_params=pltpu.CompilerParams(vmem_limit_bytes=32 << 20),
        )(*arrays)

    def own(self, slots, src_slots, sources, parts, keep=True):
        kernel = functools.partial(own_kernel, slots, src_slots, len(parts), self.scale)
        wide = pltpu.VMEM((self.segs, SRC_DEV, 2 * BINS), jnp.float32)
        out = self.kept if keep else jax.ShapeDtypeStruct(self.out, jnp.bfloat16)
        return self.call(kernel, (out, self.rows), [self.rot, self.sums, wide], *sources, *parts, self.tab)

    def more(self, slots, parts, rows, prev):
        kernel = functools.partial(more_kernel, slots, self.scale)
        return self.call(kernel, self.kept, [self.rot, self.sums], *parts, self.tab, rows, prev)

    def part(self, piece, rows):
        return self.call(part_kernel, self.sums, [self.rot], piece, self.tab, rows)

    def last(self, slot, start, piece, rows, before, prev):
        kernel = functools.partial(last_kernel, slot, start, self.scale)
        out = jax.ShapeDtypeStruct(self.out, jnp.bfloat16)
        scratch = [self.rot, self.sums, self.kept, pltpu.SemaphoreType.DMA((CENTRES,))]
        spec = pl.BlockSpec(memory_space=pl.ANY)
        return self.call(kernel, out, scratch, piece, self.tab, rows, before, prev, out_specs=spec)


def gather_sources(x):
    n = lax.axis_size("rcv")
    if n != 4:
        return [lax.all_gather(x, "rcv", axis=1, tiled=True)], [None]
    moved = [lax.ppermute(x, "rcv", [(i, i ^ k) for i in range(n)]) for k in range(1, n)]
    return [x] + moved, [lambda k=k: lax.axis_index("rcv") ^ k for k in range(n)]


def work(traces, alive, picks):
    segs, chans, samples = traces.shape
    n = lax.axis_size("src")
    n_rcv = n * chans
    early, late, whole, chosen = spectra(traces, alive, picks, SRC_DEV // lax.axis_size("rcv"), SPLIT)
    sources, src_slots = gather_sources(chosen)
    if n != 4:
        panel = lax.all_gather(whole, "src", axis=1, tiled=True)
        slots = [lambda i=i: i for i in range(4)]
        return Lags(segs, samples, n_rcv, n_rcv // 4).own(slots, src_slots, sources, [panel], keep=False)[0]

    def swap(parts, j):
        return [lax.ppermute(h, "src", [(i, i ^ j) for i in range(n)]) for h in parts]

    def slot(j):
        return lambda: lax.axis_index("src") ^ j

    far = swap([early, late], 2)
    near = swap([whole], 1)[0]
    last = swap(far, 1)
    job = Lags(segs, samples, n_rcv, chans)
    out, rows = job.own([slot(0)], src_slots, sources, [whole])
    out = job.more([slot(1)], [near], rows, out)
    out = job.more([slot(2)], far, rows, out)
    before = job.part(last[0], rows)
    return job.last(slot(3), SPLIT, last[1], rows, before, out)


def solution(mesh):
    return jax.shard_map(
        work,
        mesh=mesh,
        in_specs=(
            P(None, ("grp", "rcv", "src"), None),
            P(None, ("grp", "rcv", "src")),
            P(("grp", "rcv", "src"), None),
        ),
        out_specs=P(None, ("grp", "src"), "rcv"),
        check_vma=False,
    )
```
